256 devices in a mesh: layer: 8 (over x, y_hi), feat: 32 (over y_lo, z, core).
Axes of the slice: x: 4, y: 4 (y_hi: 2, y_lo: 2; y = y_hi * 2 + y_lo), z: 8, core: 2. Of those that a mesh axis runs over, the one named last changes fastest.
Arguments:
- inputs: bfloat16 [8, 512, 2048], P('layer', 'feat'), may hold values from -6 to 6
- targets: bfloat16 [8, 512, 2048], P('layer', 'feat'), may hold values from -6 to 6
- enc_weight: bfloat16 [8, 2048, 16384], P('layer', None, 'feat'), may hold values from -0.125 to 0.125
- enc_bias: float32 [8, 16384], P('layer', 'feat'), may hold values from -1 to 0.5
- dec_weight: bfloat16 [8, 2, 16384, 2048], P('layer', None, 'feat'), may hold values from -0.046875 to 0.046875
- dec_bias: float32 [8, 2048], P('layer'), may hold values from -3 to 3
Outputs:
- mean_loss: float32 [], replicated
- enc_grad: bfloat16 [8, 2048, 16384], P('layer', None, 'feat')
- enc_bias_grad: float32 [8, 16384], P('layer', 'feat')
- dec_grad: bfloat16 [8, 2, 16384, 2048], P('layer', None, 'feat')
- dec_bias_grad: float32 [8, 2048], P('layer')
The draws below stay inside these ranges and needn't reach their ends.
All inputs are finite; a program needn't handle non-finite values.
Results may differ from the reference program's by a relative error of at most 0.006.
Values may be sent and summed in bfloat16 or wider, within the bound.
A program may use at most 128 MiB of HBM per device.

```python
import jax
import jax.numpy as jnp

D = 2048
FEATURES = 16384
REACH = 2
TOKENS = 512
LAYERS = 8


def steps_of(rng, extent, split, smallest, top_value):
    gain = 1.0
    for axis_at, parts in split:
        steps = jax.random.uniform(jax.random.fold_in(jax.random.fold_in(rng, 6), axis_at), (parts,), jnp.float32, smallest / len(split), top_value / len(split))
        gain = gain * jnp.repeat(jnp.exp(steps), extent[axis_at] // parts).reshape((-1,) + (1,) * (len(extent) - 1 - axis_at))
    return gain


def scatter_about(rng, shape, width, reach, cuts=(), kind=jnp.bfloat16):
    loudness = steps_of(rng, shape, cuts, -0.22, 0.18) if cuts else 1.0
    result = jax.random.normal(rng, shape, jnp.float32) * width * loudness
    return jnp.minimum(jnp.maximum(result, -reach), reach).astype(kind)


def setup_inputs(seed: int = 0) -> dict:
    keys = jax.random.split(jax.random.key(seed), 7)
    return {
        "inputs": scatter_about(keys[0], (LAYERS, TOKENS, D), 1.0, 6.0, ((0, 8), (1, 32))),
        "targets": scatter_about(keys[1], (LAYERS, TOKENS, D), 1.0, 6.0, ((0, 8), (1, 32))),
        "enc_weight": scatter_about(keys[2], (LAYERS, D, FEATURES), D ** -0.5, 0.125, ((0, 8), (2, 32))),
        "enc_bias": jnp.clip(-1.0 + 1.5 * jax.random.uniform(keys[3], (LAYERS, FEATURES), jnp.float32) ** steps_of(keys[3], (LAYERS, FEATURES), ((0, 8), (1, 32)), -0.2, 0.2), -1.0, 0.5),
        "dec_weight": scatter_about(keys[4], (LAYERS, REACH, FEATURES, D), FEATURES ** -0.5, 0.046875, ((0, 8), (2, 32))),
        "dec_bias": scatter_about(keys[5], (LAYERS, D), 0.5, 3.0, ((0, 8),), jnp.float32),
    }


def reference(inputs, targets, enc_weight, enc_bias, dec_weight, dec_bias):
    pres = []
    acts = []
    for layer_idx in range(LAYERS):
        pre = jnp.dot(inputs[layer_idx], enc_weight[layer_idx], preferred_element_type=jnp.float32) + enc_bias[layer_idx]
        pres.append(pre)
        acts.append((jnp.maximum(pre, 0.0) ** 2).astype(jnp.bfloat16))
    grads = []
    for target_idx in range(LAYERS):
        recon = dec_bias[target_idx].astype(jnp.float32)
        for offset in range(REACH):
            source = target_idx - offset
            if source >= 0:
                recon = recon + jnp.dot(acts[source], dec_weight[source, offset], preferred_element_type=jnp.float32)
        grads.append((recon - targets[target_idx].astype(jnp.float32)).astype(jnp.bfloat16))
    total = jnp.float32(0.0)
    for target_idx in range(LAYERS):
        total = total + jnp.sum(grads[target_idx].astype(jnp.float32) ** 2)
    mean_loss = total / (LAYERS * TOKENS * D)
    enc_grads = []
    enc_bias_grads = []
    dec_grads = []
    dec_bias_grads = []
    for layer_idx in range(LAYERS):
        back = jnp.zeros((TOKENS, FEATURES), jnp.float32)
        per_reach = []
        for offset in range(REACH):
            target_idx = layer_idx + offset
            if target_idx < LAYERS:
                per_reach.append(jnp.dot(acts[layer_idx].T, grads[target_idx], preferred_element_type=jnp.float32).astype(jnp.bfloat16))
                back = back + jnp.dot(grads[target_idx], dec_weight[layer_idx, offset].T, preferred_element_type=jnp.float32)
            else:
                per_reach.append(jnp.zeros((FEATURES, D), jnp.bfloat16))
        dec_grads.append(jnp.stack(per_reach, axis=0))
        dpre = (back * 2.0 * jnp.maximum(pres[layer_idx], 0.0)).astype(jnp.bfloat16)
        enc_grads.append(jnp.dot(inputs[layer_idx].T, dpre, preferred_element_type=jnp.float32).astype(jnp.bfloat16))
        enc_bias_grads.append(jnp.sum(dpre.astype(jnp.float32), axis=0))
        dec_bias_grads.append(jnp.sum(grads[layer_idx].astype(jnp.float32), axis=0))
    return (mean_loss, jnp.stack(enc_grads, 0), jnp.stack(enc_bias_grads, 0), jnp.stack(dec_grads, 0), jnp.stack(dec_bias_grads, 0))
```

```python
import jax
import jax.numpy as jnp
from jax import lax
from jax.experimental import pallas as pl
from jax.experimental.pallas import tpu as pltpu
from jax.sharding import Mesh
from jax.sharding import PartitionSpec as P

MESH = pl.DeviceIdType.MESH
BF16, F32 = jnp.bfloat16, jnp.float32
LAYER = ("x", "yh")
FEAT = ("yl", "z", "c")
NX, NZ = 4, 8

BLOCKS = (
    ((0, 0), (1, 0), (0, 1), (0, -1)),
    ((0, 2), (0, -2), (1, 1), (1, -1)),
    ((0, 3), (0, -3), (1, 2), (1, -2)),
    ((0, 4), (1, 3), (1, -3), (1, 4)),
)
PLACE = {slot: (b, k) for b, block in enumerate(BLOCKS) for k, slot in enumerate(block)}
OWN = (0, 0)
WAVES = (
    (OWN,),
    ((0, 1), (0, -1), (1, 0)),
    ((0, 2), (0, -2), (1, 1), (1, -1)),
    ((0, 3), (0, -3), (1, 2), (1, -2)),
    ((0, 4), (1, 3), (1, -3)),
    ((1, 4),),
)


def parent_of(slot, half):
    dy, dz = slot
    if dy == 1 and dz in (0, 3, -3, 4):
        return (0, dz), "y"
    if dz == 4:
        return ((0, 3), "+") if half == 0 else ((0, -3), "-")
    return ((dy, dz - 1), "+") if dz > 0 else ((dy, dz + 1), "-")


SLOTS = tuple(slot for block in BLOCKS for slot in block)
CHILDREN = {
    (half, slot): tuple(c for c in SLOTS if c != OWN and parent_of(c, half)[0] == slot)
    for half in (0, 1)
    for slot in SLOTS
}


def mirrored(slot, half):
    dy, dz = slot
    return (dy, dz) if half == 0 or dz == 4 else (dy, -dz)


REDUCE = (
    ((1, 4), (1, 3), (1, -3), (1, 2), (1, -2)),
    ((0, 4), (0, -3), (1, 1), (1, -1)),
    ((0, 3), (0, -2), (1, 0)),
    ((0, 2), (0, -1)),
    ((0, 1),),
)


def main_kernel(
    x_hbm, t_hbm, ew_hbm, eb_hbm, dw_hbm, db_hbm,
    tok_o, acts_o, grads_o, dpre_o, sums_o, loss_o,
    tok, ew, dw, eb, db, tg, pre, acts, part, sib_out, sib_in, arr, snd, shift_out, shift_in,
    gshift_in, gr, back, dpre, sums, squares, loss_all, loss_sum,
    load_sem, store_sem, tok_s, tok_r, tsib_s, tsib_r, psib_s, psib_r, red_s, red_r,
    sh_s, sh_r, gr_s, gr_r, gsib_s, gsib_r, loss_s, loss_r,
):
    x, yh = lax.axis_index("x"), lax.axis_index("yh")
    yl, z, c = lax.axis_index("yl"), lax.axis_index("z"), lax.axis_index("c")
    layer = x * 2 + yh
    width = dw.shape[2]
    half_width = width // 2

    to = {
        "+": {"z": lax.rem(z + 1, NZ)},
        "-": {"z": lax.rem(z + NZ - 1, NZ)},
        "y": {"yl": 1 - yl},
    }
    back_to = {"+": to["-"], "-": to["+"], "y": to["y"]}
    sibling = {"c": 1 - c}
    following = {"x": lax.rem(x + yh, NX), "yh": 1 - yh}
    previous = {"x": lax.rem(x + yh + NX - 1, NX), "yh": 1 - yh}
    peers = [
        {"x": lax.rem(x + k // 2, NX), "yh": lax.rem(yh + k % 2, 2)} for k in range(1, 2 * NX)
    ]

    def load(k, src, dst):
        copy = pltpu.make_async_copy(src, dst, load_sem.at[k])
        copy.start()
        return copy

    own_loads = [
        load(h, x_hbm.at[0, :, pl.ds(h * half_width, half_width)], tok.at[h, 0, 0, 0])
        for h in (0, 1)
    ]
    ew_load = load(2, ew_hbm.at[0], ew)
    eb_load = load(3, eb_hbm, eb)
    dw_loads = [load(4 + r, dw_hbm.at[0, r], dw.at[r]) for r in (1, 0)]
    tg_load = load(6, t_hbm.at[0], tg)
    db_load = load(7, db_hbm, db)

    barrier = pltpu.get_barrier_semaphore()
    greeted = [to["+"], to["-"], to["y"], sibling, following, previous, *peers]
    for device in greeted:
        pl.semaphore_signal(barrier, inc=1, device_id=device, device_id_type=MESH)
    pl.semaphore_wait(barrier, len(greeted))

    def remote(src, dst, send_sem, recv_sem, device):
        return pltpu.make_async_remote_copy(
            src_ref=src, dst_ref=dst, send_sem=send_sem, recv_sem=recv_sem,
            device_id=device, device_id_type=MESH,
        )

    sent = []

    def gather(buf, ici_s, ici_r, sib_s, sib_r):
        ici, sib = {}, {}
        for h in (0, 1):
            for s in SLOTS:
                b, k = PLACE[s]
                sib[h, s] = remote(
                    buf.at[h, b, 0, k], buf.at[h, b, 1, k],
                    sib_s.at[h, b, k], sib_r.at[h, b, k], sibling,
                )
                if s == OWN:
                    continue
                parent, way = parent_of(s, h)
                pb, pk = PLACE[parent]
                ici[h, s] = remote(
                    buf.at[h, pb, 0, pk], buf.at[h, b, 0, k],
                    ici_s.at[h, b, k], ici_r.at[h, b, k], to[way],
                )

        def stage(n, h):
            for s in WAVES[n]:
                if s != OWN:
                    ici[h, s].wait_recv()
                for child in CHILDREN[h, s]:
                    ici[h, child].start()
                    sent.append(ici[h, child])
                sib[h, s].start()
                sent.append(sib[h, s])

        def settle(b, h):
            for s in BLOCKS[b]:
                sib[h, s].wait_recv()

        return stage, settle

    stage, settle = gather(tok, tok_s, tok_r, tsib_s, tsib_r)

    def encode(b):
        rows = pl.ds(b * 128, 128)
        for h in (0, 1):
            settle(b, h)
        value = eb[...] + jnp.zeros((128, 1), F32)
        for h in (0, 1):
            value += jnp.dot(
                tok[h, b].reshape(128, half_width),
                ew[h * half_width : (h + 1) * half_width],
                preferred_element_type=F32,
            )
        value = jnp.maximum(value, 0.0)
        pre[rows] = value
        acts[rows] = (value * value).astype(BF16)

    for h in (0, 1):
        own_loads[h].wait()
        stage(0, h)
    for n in (1, 2):
        for h in (0, 1):
            stage(n, h)
    ew_load.wait()
    eb_load.wait()
    encode(0)
    for n in (3, 4, 5):
        for h in (0, 1):
            stage(n, h)
        encode(n - 2)
    stores = []

    def store(src, dst):
        copy = pltpu.make_async_copy(src, dst, store_sem.at[len(stores)])
        copy.start()
        stores.append(copy)

    store(tok, tok_o)
    store(acts, acts_o)

    psib = {
        (h, b): remote(
            sib_out.at[h, b], sib_in.at[h, b], psib_s.at[h, b], psib_r.at[h, b], sibling
        )
        for h in (0, 1)
        for b in range(4)
    }
    tile = 512

    def decode(b):
        lhs = acts[pl.ds(b * 128, 128)]
        for h in (0, 1):

            @pl.loop(0, width // tile)
            def _(j):
                columns = pl.ds(pl.multiple_of(j * tile, tile), tile)
                value = jnp.dot(lhs, dw[1 - h, :, columns], preferred_element_type=F32)
                part[h, b, :, :, columns] = value[:64].reshape(4, 16, tile)
                sib_out[h, b, :, :, columns] = value[64:].astype(BF16).reshape(4, 16, tile)

            psib[h, b].start()
            sent.append(psib[h, b])

    red = {}
    for h in (0, 1):
        for s in SLOTS[1:]:
            b, k = PLACE[s]
            red[h, s] = remote(
                snd.at[h, b, k], arr.at[h, b, k], red_s.at[h, b, k], red_r.at[h, b, k],
                back_to[parent_of(s, h)[1]],
            )

    def total(h, s):
        b, k = PLACE[s]
        value = part[h, b, k] + sib_in[h, b, k].astype(F32)
        for child in CHILDREN[h, s]:
            red[h, child].wait_recv()
            cb, ck = PLACE[child]
            value += arr[h, cb, ck].astype(F32)
        return value

    def pass_on(h, s):
        b, k = PLACE[s]
        snd[h, b, k] = total(h, s).astype(BF16)
        red[h, s].start()
        sent.append(red[h, s])

    for load_ in dw_loads:
        load_.wait()
    decode(3)
    decode(2)
    for h in (0, 1):
        psib[h, 3].wait_recv()
        psib[h, 2].wait_recv()
        for s in REDUCE[0]:
            pass_on(h, mirrored(s, h))
    decode(1)
    for h in (0, 1):
        psib[h, 1].wait_recv()
        for s in REDUCE[1]:
            pass_on(h, mirrored(s, h))
    decode(0)
    for h in (0, 1):
        psib[h, 0].wait_recv()
        for s in REDUCE[2]:
            pass_on(h, mirrored(s, h))
    for n in (3, 4):
        for h in (0, 1):
            for s in REDUCE[n]:
                pass_on(h, mirrored(s, h))
    shift_out[...] = total(0, OWN).astype(BF16)
    shift = remote(shift_out, shift_in, sh_s.at[0], sh_r.at[0], following)
    shift.start()
    tg_load.wait()
    db_load.wait()
    recon = total(1, OWN) + db[...] - tg[...].astype(F32)
    shift.wait_recv()
    recon += jnp.where(layer == 0, 0.0, shift_in[...].astype(F32))
    gr[0, 0, 0, 0] = recon.astype(BF16)
    gshift = remote(gr.at[0, 0, 0, 0], gshift_in, sh_s.at[1], sh_r.at[1], previous)
    gshift.start()
    sent += [shift, gshift]

    stage, settle = gather(gr, gr_s, gr_r, gsib_s, gsib_r)

    def through(b, h):
        rows = pl.ds(b * 128, 128)
        settle(b, h)
        value = lax.dot_general(
            gr[h, b].reshape(128, width), dw[h], (((1,), (1,)), ((), ())),
            preferred_element_type=F32,
        )
        if h == 0:
            back[rows] = value
        else:
            value += back[rows]
            dpre[rows] = (value * 2.0 * pre[rows]).astype(BF16)

    def add_up():
        @pl.loop(0, width // tile)
        def _(j):
            columns = pl.ds(pl.multiple_of(j * tile, tile), tile)
            total_sum = jnp.zeros((8, tile), F32)
            total_sq = jnp.zeros((8, tile), F32)
            for b in range(4):
                for p in range(2):
                    value = gr[0, b, p, :, :, columns].astype(F32).reshape(8, 8, tile)
                    total_sum += jnp.sum(value, axis=0)
                    total_sq += jnp.sum(value * value, axis=0)
            sums[:, columns] = total_sum
            squares[:, columns] = total_sq

        value = jnp.zeros((8, 128), F32)
        for j in range(width // 128):
            value += squares[:, j * 128 : (j + 1) * 128]
        loss_all[0] = value
        store(sums, sums_o)

    stage(0, 0)
    stage(1, 0)
    gshift.wait_recv()
    gr[1, 0, 0, 0] = jnp.where(layer == 2 * NX - 1, 0.0, gshift_in[...].astype(F32)).astype(BF16)
    stage(0, 1)
    stage(2, 0)
    stage(1, 1)
    through(0, 0)
    stage(3, 0)
    stage(2, 1)
    through(1, 0)
    stage(4, 0)
    stage(3, 1)
    through(2, 0)
    stage(5, 0)
    through(0, 1)
    stage(4, 1)
    through(3, 0)
    store(gr.at[0], grads_o.at[0])
    stage(5, 1)
    add_up()
    tells = []
    for k, device in enumerate(peers):
        tells.append(
            remote(loss_all.at[0], loss_all.at[k + 1], loss_s.at[k], loss_r.at[k], device)
        )
        tells[-1].start()
    for b in (1, 2, 3):
        through(b, 1)
    store(gr.at[1], grads_o.at[1])
    store(dpre, dpre_o)
    for tell in tells:
        tell.wait_recv()
    sent += tells
    value = loss_all[0]
    for k in range(1, 2 * NX):
        value += loss_all[k]
    loss_sum[...] = value
    store(loss_sum, loss_o)
    for copy in sent:
        copy.wait_send()
    for copy in stores:
        copy.wait()


def grad_kernel(scale, tok, acts, dpre, grads, sums, loss, eg, ebg, dg, dbg, mean):
    contract = (((0,), (0,)), ((), ()))
    eg[0] = lax.dot_general(tok[0], dpre[...], contract, preferred_element_type=F32).astype(BF16)
    dg[0, 0] = lax.dot_general(acts[...], grads[0], contract, preferred_element_type=F32).astype(
        BF16
    )

    @pl.when(pl.program_id(0) == 0)
    def _():
        ebg[...] = jnp.sum(dpre[...].astype(F32), axis=0, keepdims=True)
        dbg[...] = jnp.sum(sums[...], axis=0, keepdims=True)
        mean[0, 0] = jnp.sum(loss[...]) * scale


def shards(inputs, targets, enc_weight, enc_bias, dec_weight, dec_bias):
    rows, width = inputs.shape[1:]
    feats = enc_weight.shape[2]
    tokens = rows * 32
    half_width = width // 2
    anywhere = pl.BlockSpec(memory_space=pl.ANY)
    dma = pltpu.SemaphoreType.DMA
    tok, acts, grads, dpre, sums, loss = pl.pallas_call(
        main_kernel,
        out_shape=(
            jax.ShapeDtypeStruct((2, 4, 2, 4, rows, half_width), BF16),
            jax.ShapeDtypeStruct((tokens, feats), BF16),
            jax.ShapeDtypeStruct((2, 4, 2, 4, rows, width), BF16),
            jax.ShapeDtypeStruct((tokens, feats), BF16),
            jax.ShapeDtypeStruct((8, width), F32),
            jax.ShapeDtypeStruct((8, 128), F32),
        ),
        in_specs=[anywhere] * 6,
        out_specs=(anywhere,) * 6,
        scratch_shapes=[
            pltpu.VMEM((2, 4, 2, 4, rows, half_width), BF16),
            pltpu.VMEM((width, feats), BF16),
            pltpu.VMEM((2, feats, width), BF16),
            pltpu.VMEM((1, feats), F32),
            pltpu.VMEM((1, width), F32),
            pltpu.VMEM((rows, width), BF16),
            pltpu.VMEM((tokens, feats), F32),
            pltpu.VMEM((tokens, feats), BF16),
            pltpu.VMEM((2, 4, 4, rows, width), F32),
            pltpu.VMEM((2, 4, 4, rows, width), BF16),
            pltpu.VMEM((2, 4, 4, rows, width), BF16),
            pltpu.VMEM((2, 4, 4, rows, width), BF16),
            pltpu.VMEM((2, 4, 4, rows, width), BF16),
            pltpu.VMEM((rows, width), BF16),
            pltpu.VMEM((rows, width), BF16),
            pltpu.VMEM((rows, width), BF16),
            pltpu.VMEM((2, 4, 2, 4, rows, width), BF16),
            pltpu.VMEM((tokens, feats), F32),
            pltpu.VMEM((tokens, feats), BF16),
            pltpu.VMEM((8, width), F32),
            pltpu.VMEM((8, width), F32),
            pltpu.VMEM((2 * NX, 8, 128), F32),
            pltpu.VMEM((8, 128), F32),
            dma((8,)),
            dma((8,)),
            *[dma((2, 4, 4))] * 4,
            *[dma((2, 4))] * 2,
            *[dma((2, 4, 4))] * 2,
            *[dma((2,))] * 2,
            *[dma((2, 4, 4))] * 4,
            *[dma((2 * NX - 1,))] * 2,
        ],
        compiler_params=pltpu.CompilerParams(
            collective_id=0, has_side_effects=True, vmem_limit_bytes=60 * 2**20
        ),
        name="exchange",
    )(inputs, targets, enc_weight, enc_bias, dec_weight, dec_bias)
    tok = tok.reshape(2, tokens, half_width)
    grads = grads.reshape(2, tokens, width)
    whole = lambda *shape: pl.BlockSpec(shape, lambda i: (0,) * len(shape))
    eg, ebg, dg, dbg, mean = pl.pallas_call(
        lambda *refs: grad_kernel(1.0 / (2 * NX * tokens * width), *refs),
        grid=(8,),
        out_shape=(
            jax.ShapeDtypeStruct((1, width, feats), BF16),
            jax.ShapeDtypeStruct((1, feats), F32),
            jax.ShapeDtypeStruct((1, 2, feats, width), BF16),
            jax.ShapeDtypeStruct((1, width), F32),
            jax.ShapeDtypeStruct((1, 1), F32),
        ),
        in_specs=[
            pl.BlockSpec((1, tokens, width // 8), lambda i: (i // 4, 0, i % 4)),
            whole(tokens, feats),
            whole(tokens, feats),
            pl.BlockSpec((1, tokens, width // 4), lambda i: (i // 4, 0, i % 4)),
            whole(8, width),
            whole(8, 128),
        ],
        out_specs=(
            pl.BlockSpec((1, width // 8, feats), lambda i: (0, i, 0)),
            whole(1, feats),
            pl.BlockSpec((1, 1, feats, width // 4), lambda i: (0, i // 4, 0, i % 4)),
            whole(1, width),
            pl.BlockSpec(memory_space=pltpu.SMEM),
        ),
        name="weight_grads",
    )(tok, acts, dpre, grads, sums, loss)
    return mean[0, 0], eg, ebg, dg, dbg


def solution(mesh):
    finer = Mesh(mesh.devices.reshape(NX, 2, 2, NZ, 2), LAYER + FEAT)
    return jax.shard_map(
        shards,
        mesh=finer,
        in_specs=(
            P(LAYER, FEAT, None),
            P(LAYER, FEAT, None),
            P(LAYER, None, FEAT),
            P(LAYER, FEAT),
            P(LAYER, None, FEAT, None),
            P(LAYER, None),
        ),
        out_specs=(
            P(),
            P(LAYER, None, FEAT),
            P(LAYER, FEAT),
            P(LAYER, None, FEAT, None),
            P(LAYER, None),
        ),
        check_vma=False,
    )
```

```python
import jax
import jax.numpy as jnp
from jax import lax
from jax.experimental import pallas as pl
from jax.experimental.pallas import tpu as pltpu
from jax.sharding import Mesh
from jax.sharding import PartitionSpec as P

MESH = pl.DeviceIdType.MESH
BF16, F32 = jnp.bfloat16, jnp.float32
LAYER = ("x", "yh")
FEAT = ("yl", "z", "c")
NX, NZ = 4, 8

BLOCKS = (
    ((0, 0), (1, 0), (0, 1), (0, -1)),
    ((0, 2), (0, -2), (1, 1), (1, -1)),
    ((1, 2), (1, -2), (0, 3), (0, -3)),
    ((0, 4), (1, 3), (1, -3), (1, 4)),
)
SLOTS = tuple(slot for block in BLOCKS for slot in block)
PLACE = {slot: (b, k) for b, block in enumerate(BLOCKS) for k, slot in enumerate(block)}
OWN = (0, 0)


def own_tree(half, far):
    edges = {
        (0, 2): (OWN, "++"), (0, -2): (OWN, "--"), (1, 0): (OWN, "y"),
        (0, 1): (OWN, "+"), (0, -1): (OWN, "-"),
        (0, 3): ((0, 2), "+"), (0, -3): ((0, -2), "-"),
        (0, 4): ((0, 2), "++") if far == "+" else ((0, -2), "--"),
        (1, 1): ((1, 0), "+"), (1, -1): ((1, 0), "-"),
        (1, 2): ((0, 2), "y"), (1, -2): ((0, -2), "y"),
        (1, 3): ((0, 3), "y"), (1, -3): ((0, -3), "y"), (1, 4): ((0, 4), "y"),
    }
    return {(half, s): ((half, p), way) for s, (p, way) in edges.items()}


def next_tree():
    crossing = {(1, 2): (0, 2), (1, -2): (0, -2), (0, 0): (1, 0), (1, 0): (0, 0),
                (1, 1): (0, 1), (1, -1): (0, -1)}
    edges = {
        (1, 3): ((1, 2), "+"), (1, -3): ((1, -2), "-"), (1, 4): ((1, -2), "--"),
        (0, 1): ((0, 0), "+"), (0, -1): ((0, 0), "-"),
        (0, 2): ((0, 1), "+"), (0, -2): ((0, -1), "-"),
        (0, 3): ((1, 3), "y"), (0, -3): ((1, -3), "y"), (0, 4): ((1, 4), "y"),
    }
    return {(1, s): ((0, p), "cross") for s, p in crossing.items()} | {
        (1, s): ((1, p), way) for s, (p, way) in edges.items()
    }


INPUT_TREE = own_tree(0, "+") | own_tree(1, "-")
ERROR_TREE = next_tree() | own_tree(0, "+")
OWN_WAVES = (
    (OWN,),
    ((0, 2), (0, -2), (1, 0), (0, 1), (0, -1)),
    ((0, 3), (0, -3), (0, 4), (1, 1), (1, -1), (1, 2), (1, -2)),
    ((1, 3), (1, -3), (1, 4)),
)
NEXT_WAVES = (
    ((1, 0),),
    ((1, 2), (1, -2), (0, 0), (1, 1), (1, -1)),
    ((1, 3), (1, -3), (1, 4), (0, 1), (0, -1)),
    ((0, 3), (0, -3), (0, 4), (0, 2), (0, -2)),
)


def children_of(tree, node):
    return tuple(child for child, (parent, _) in tree.items() if parent == node)


def main_kernel(
    x_hbm, t_hbm, ew_hbm, eb_hbm, dw_hbm, db_hbm,
    tok_o, acts_o, grads_o, dpre_o, sums_o, loss_o,
    tok, ew, dw, eb, db, tg, pre, acts, part, sib_out, sib_in, arr, snd, zeros, gr, back, dpre, sums, squares, loss_all, loss_sum,
    load_sem, store_sem, tok_s, tok_r, tsib_s, tsib_r, psib_s, psib_r, red_s, red_r,
    gr_s, gr_r, gsib_s, gsib_r, loss_s, loss_r,
):
    x, yh = lax.axis_index("x"), lax.axis_index("yh")
    yl, z, c = lax.axis_index("yl"), lax.axis_index("z"), lax.axis_index("c")
    layer = x * 2 + yh
    width = dw.shape[2]
    half_width = width // 2

    to = {
        "+": {"z": lax.rem(z + 1, NZ)},
        "++": {"z": lax.rem(z + 2, NZ)},
        "-": {"z": lax.rem(z + NZ - 1, NZ)},
        "--": {"z": lax.rem(z + NZ - 2, NZ)},
        "y": {"yl": 1 - yl},
        "cross": {"x": lax.rem(x + yh + NX - 1, NX), "yh": 1 - yh, "yl": 1 - yl},
    }
    back_to = {
        "+": to["-"], "++": to["--"], "-": to["+"], "--": to["++"], "y": to["y"],
        "cross": {"x": lax.rem(x + yh, NX), "yh": 1 - yh, "yl": 1 - yl},
    }
    sibling = {"c": 1 - c}
    peers = [
        {"x": lax.rem(x + k // 2, NX), "yh": lax.rem(yh + k % 2, 2)} for k in range(1, 2 * NX)
    ]

    def load(k, src, dst):
        copy = pltpu.make_async_copy(src, dst, load_sem.at[k])
        copy.start()
        return copy

    zeros[...] = jnp.zeros_like(zeros)
    own_loads = [
        load(h, x_hbm.at[0, :, pl.ds(h * half_width, half_width)], tok.at[h, 0, 0, 0])
        for h in (0, 1)
    ]
    ew_load = load(2, ew_hbm.at[0], ew)
    eb_load = load(3, eb_hbm, eb)
    dw_loads = [load(4 + r, dw_hbm.at[0, r], dw.at[r]) for r in (1, 0)]
    tg_load = load(6, t_hbm.at[0], tg)
    db_load = load(7, db_hbm, db)

    barrier = pltpu.get_barrier_semaphore()
    greeted = [*to.values(), back_to["cross"], sibling, *peers]
    for device in greeted:
        pl.semaphore_signal(barrier, inc=1, device_id=device, device_id_type=MESH)
    pl.semaphore_wait(barrier, len(greeted))

    def remote(src, dst, send_sem, recv_sem, device):
        return pltpu.make_async_remote_copy(
            src_ref=src, dst_ref=dst, send_sem=send_sem, recv_sem=recv_sem,
            device_id=device, device_id_type=MESH,
        )

    sent = []

    def gather(tree, buf, ici_s, ici_r, sib_s, sib_r):
        ici, sib = {}, {}
        for h in (0, 1):
            for s in SLOTS:
                b, k = PLACE[s]
                sib[h, s] = remote(
                    buf.at[h, b, 0, k], buf.at[h, b, 1, k],
                    sib_s.at[h, b, k], sib_r.at[h, b, k], sibling,
                )

        def hop(node):
            (ph, parent), way = tree[node]
            h, s = node
            b, k = PLACE[s]
            pb, pk = PLACE[parent]
            sems = ici_s.at[h, b, k], ici_r.at[h, b, k]
            ici[node] = remote(buf.at[ph, pb, 0, pk], buf.at[h, b, 0, k], *sems, to[way])
            if way == "cross":
                blank = remote(zeros, buf.at[h, b, 0, k], *sems, to[way])
                pl.when(layer == 0)(blank.start)
                pl.when(layer != 0)(ici[node].start)
            else:
                ici[node].start()
            sent.append(ici[node])

        def stage(h, slots):
            for s in slots:
                if (h, s) in tree:
                    ici[h, s].wait_recv()
                for child in children_of(tree, (h, s)):
                    hop(child)
                sib[h, s].start()
                sent.append(sib[h, s])

        def settle(h, b):
            for s in BLOCKS[b]:
                sib[h, s].wait_recv()

        return stage, settle

    stage, settle = gather(INPUT_TREE, tok, tok_s, tok_r, tsib_s, tsib_r)

    def encode(b):
        rows = pl.ds(b * 128, 128)
        for h in (0, 1):
            settle(h, b)
        value = eb[...] + jnp.zeros((128, 1), F32)
        for h in (0, 1):
            value += jnp.dot(
                tok[h, b].reshape(128, half_width),
                ew[h * half_width : (h + 1) * half_width],
                preferred_element_type=F32,
            )
        value = jnp.maximum(value, 0.0)
        pre[rows] = value
        acts[rows] = (value * value).astype(BF16)

    for h in (0, 1):
        own_loads[h].wait()
        stage(h, OWN_WAVES[0])
    for h in (0, 1):
        stage(h, OWN_WAVES[1])
    ew_load.wait()
    eb_load.wait()
    encode(0)
    for h in (0, 1):
        stage(h, OWN_WAVES[2])
    encode(1)
    encode(2)
    for h in (0, 1):
        stage(h, OWN_WAVES[3])
    encode(3)
    stores = []

    def store(src, dst):
        copy = pltpu.make_async_copy(src, dst, store_sem.at[len(stores)])
        copy.start()
        stores.append(copy)

    store(tok, tok_o)
    store(acts, acts_o)

    psib = {
        (h, p): remote(
            sib_out.at[h, pl.ds(2 * p, 2)], sib_in.at[h, pl.ds(2 * p, 2)],
            psib_s.at[h, p], psib_r.at[h, p], sibling,
        )
        for h in (0, 1)
        for p in (0, 1)
    }
    tile = 512

    def decode(p):
        for h in (1, 0):

            @pl.loop(0, width // tile)
            def _(j):
                columns = pl.ds(pl.multiple_of(j * tile, tile), tile)
                value = jnp.dot(
                    acts[pl.ds(p * 256, 256)], dw[h, :, columns], preferred_element_type=F32
                ).reshape(2, 2, 4, 16, tile)
                for b in (0, 1):
                    part[h, 2 * p + b, :, :, columns] = value[b, 0]
                    sib_out[h, 2 * p + b, :, :, columns] = value[b, 1].astype(BF16)

            psib[h, p].start()
            sent.append(psib[h, p])

    red = {}
    for (h, s), (_, way) in ERROR_TREE.items():
        b, k = PLACE[s]
        red[h, s] = remote(
            snd.at[h, b, k], arr.at[h, b, k], red_s.at[h, b, k], red_r.at[h, b, k], back_to[way]
        )

    def total(h, s):
        b, k = PLACE[s]
        value = part[h, b, k] + sib_in[h, b, k].astype(F32)
        for child in children_of(ERROR_TREE, (h, s)):
            red[child].wait_recv()
            cb, ck = PLACE[child[1]]
            term = arr[child[0], cb, ck].astype(F32)
            if ERROR_TREE[child][1] == "cross":
                term = jnp.where(layer == 0, 0.0, term)
            value += term
        return value

    def pass_on(h, *slots):
        for s in slots:
            b, k = PLACE[s]
            snd[h, b, k] = total(h, s).astype(BF16)
            red[h, s].start()
            sent.append(red[h, s])

    for load_ in dw_loads:
        load_.wait()
    decode(1)
    psib[1, 1].wait_recv()
    pass_on(1, (0, 3), (0, -3), (0, 4))
    psib[0, 1].wait_recv()
    pass_on(0, (1, 3), (1, -3), (1, 4), (1, 2), (1, -2))
    decode(0)
    psib[1, 0].wait_recv()
    pass_on(1, (0, 2), (0, -2), (1, 3), (1, -3), (1, 4), (1, 1), (1, -1), (1, 0))
    psib[0, 0].wait_recv()
    pass_on(0, (1, 1), (1, -1), (0, 3), (0, -3), (0, 4))
    pass_on(1, (0, 1), (0, -1), (1, 2), (1, -2), (0, 0))
    tg_load.wait()
    db_load.wait()
    pass_on(0, (0, 1), (0, -1), (0, 2), (0, -2), (1, 0))
    gr[0, 0, 0, 0] = (total(0, OWN) + db[...] - tg[...].astype(F32)).astype(BF16)

    stage, settle = gather(ERROR_TREE, gr, gr_s, gr_r, gsib_s, gsib_r)

    def through(h):
        for b in range(4):
            settle(h, b)
        return lax.dot_general(
            gr[h].reshape(512, width), dw[h], (((1,), (1,)), ((), ())), preferred_element_type=F32
        )

    def add_up():
        @pl.loop(0, width // tile)
        def _(j):
            columns = pl.ds(pl.multiple_of(j * tile, tile), tile)
            total_sum = jnp.zeros((8, tile), F32)
            total_sq = jnp.zeros((8, tile), F32)
            for b in range(4):
                for p in range(2):
                    value = gr[0, b, p, :, :, columns].astype(F32).reshape(8, 8, tile)
                    total_sum += jnp.sum(value, axis=0)
                    total_sq += jnp.sum(value * value, axis=0)
            sums[:, columns] = total_sum
            squares[:, columns] = total_sq

        value = jnp.zeros((8, 128), F32)
        for j in range(width // 128):
            value += squares[:, j * 128 : (j + 1) * 128]
        loss_all[0] = value
        store(sums, sums_o)

    stage(0, OWN_WAVES[0])
    stage(0, OWN_WAVES[1])
    stage(1, NEXT_WAVES[0])
    stage(0, OWN_WAVES[2])
    stage(1, NEXT_WAVES[1])
    stage(0, OWN_WAVES[3])
    stage(1, NEXT_WAVES[2])
    back[...] = through(0)
    add_up()
    tells = []
    for k, device in enumerate(peers):
        tells.append(
            remote(loss_all.at[0], loss_all.at[k + 1], loss_s.at[k], loss_r.at[k], device)
        )
        tells[-1].start()
    store(gr.at[0], grads_o.at[0])
    stage(1, NEXT_WAVES[3])
    dpre[...] = ((through(1) + back[...]) * 2.0 * pre[...]).astype(BF16)
    store(gr.at[1], grads_o.at[1])
    store(dpre, dpre_o)
    for tell in tells:
        tell.wait_recv()
    sent += tells
    value = loss_all[0]
    for k in range(1, 2 * NX):
        value += loss_all[k]
    loss_sum[...] = value
    store(loss_sum, loss_o)
    for copy in sent:
        copy.wait_send()
    for copy in stores:
        copy.wait()


def grad_kernel(scale, tok, acts, dpre, grads, sums, loss, eg, ebg, dg, dbg, mean):
    contract = (((0,), (0,)), ((), ()))
    eg[0] = lax.dot_general(tok[0], dpre[...], contract, preferred_element_type=F32).astype(BF16)
    for r in (0, 1):
        dg[0, r] = lax.dot_general(
            acts[...], grads[r], contract, preferred_element_type=F32
        ).astype(BF16)

    @pl.when(pl.program_id(0) == 0)
    def _():
        ebg[...] = jnp.sum(dpre[...].astype(F32), axis=0, keepdims=True)
        dbg[...] = jnp.sum(sums[...], axis=0, keepdims=True)
        mean[0, 0] = jnp.sum(loss[...]) * scale


def shards(inputs, targets, enc_weight, enc_bias, dec_weight, dec_bias):
    rows, width = inputs.shape[1:]
    feats = enc_weight.shape[2]
    tokens = rows * 32
    half_width = width // 2
    anywhere = pl.BlockSpec(memory_space=pl.ANY)
    dma = pltpu.SemaphoreType.DMA
    tok, acts, grads, dpre, sums, loss = pl.pallas_call(
        main_kernel,
        out_shape=(
            jax.ShapeDtypeStruct((2, 4, 2, 4, rows, half_width), BF16),
            jax.ShapeDtypeStruct((tokens, feats), BF16),
            jax.ShapeDtypeStruct((2, 4, 2, 4, rows, width), BF16),
            jax.ShapeDtypeStruct((tokens, feats), BF16),
            jax.ShapeDtypeStruct((8, width), F32),
            jax.ShapeDtypeStruct((8, 128), F32),
        ),
        in_specs=[anywhere] * 6,
        out_specs=(anywhere,) * 6,
        scratch_shapes=[
            pltpu.VMEM((2, 4, 2, 4, rows, half_width), BF16),
            pltpu.VMEM((width, feats), BF16),
            pltpu.VMEM((2, feats, width), BF16),
            pltpu.VMEM((1, feats), F32),
            pltpu.VMEM((1, width), F32),
            pltpu.VMEM((rows, width), BF16),
            pltpu.VMEM((tokens, feats), F32),
            pltpu.VMEM((tokens, feats), BF16),
            pltpu.VMEM((2, 4, 4, rows, width), F32),
            pltpu.VMEM((2, 4, 4, rows, width), BF16),
            pltpu.VMEM((2, 4, 4, rows, width), BF16),
            pltpu.VMEM((2, 4, 4, rows, width), BF16),
            pltpu.VMEM((2, 4, 4, rows, width), BF16),
            pltpu.VMEM((rows, width), BF16),
            pltpu.VMEM((2, 4, 2, 4, rows, width), BF16),
            pltpu.VMEM((tokens, feats), F32),
            pltpu.VMEM((tokens, feats), BF16),
            pltpu.VMEM((8, width), F32),
            pltpu.VMEM((8, width), F32),
            pltpu.VMEM((2 * NX, 8, 128), F32),
            pltpu.VMEM((8, 128), F32),
            dma((8,)),
            dma((8,)),
            *[dma((2, 4, 4))] * 4,
            *[dma((2, 2))] * 2,
            *[dma((2, 4, 4))] * 2,
            *[dma((2, 4, 4))] * 4,
            *[dma((2 * NX - 1,))] * 2,
        ],
        compiler_params=pltpu.CompilerParams(
            collective_id=0, has_side_effects=True, vmem_limit_bytes=60 * 2**20
        ),
        name="exchange",
    )(inputs, targets, enc_weight, enc_bias, dec_weight, dec_bias)
    tok = tok.reshape(2, tokens, half_width)
    grads = grads.reshape(2, tokens, width)
    whole = lambda *shape: pl.BlockSpec(shape, lambda i: (0,) * len(shape))
    eg, ebg, dg, dbg, mean = pl.pallas_call(
        lambda *refs: grad_kernel(1.0 / (2 * NX * tokens * width), *refs),
        grid=(4,),
        out_shape=(
            jax.ShapeDtypeStruct((1, width, feats), BF16),
            jax.ShapeDtypeStruct((1, feats), F32),
            jax.ShapeDtypeStruct((1, 2, feats, width), BF16),
            jax.ShapeDtypeStruct((1, width), F32),
            jax.ShapeDtypeStruct((1, 1), F32),
        ),
        in_specs=[
            pl.BlockSpec((1, tokens, width // 4), lambda i: (i // 2, 0, i % 2)),
            whole(tokens, feats),
            whole(tokens, feats),
            pl.BlockSpec((2, tokens, width // 4), lambda i: (0, 0, i)),
            whole(8, width),
            whole(8, 128),
        ],
        out_specs=(
            pl.BlockSpec((1, width // 4, feats), lambda i: (0, i, 0)),
            whole(1, feats),
            pl.BlockSpec((1, 2, feats, width // 4), lambda i: (0, 0, 0, i)),
            whole(1, width),
            pl.BlockSpec(memory_space=pltpu.SMEM),
        ),
        name="weight_grads",
    )(tok, acts, dpre, grads, sums, loss)
    return mean[0, 0], eg, ebg, dg, dbg


def solution(mesh):
    finer = Mesh(mesh.devices.reshape(NX, 2, 2, NZ, 2), LAYER + FEAT)
    return jax.shard_map(
        shards,
        mesh=finer,
        in_specs=(
            P(LAYER, FEAT, None),
            P(LAYER, FEAT, None),
            P(LAYER, None, FEAT),
            P(LAYER, FEAT),
            P(LAYER, None, FEAT, None),
            P(LAYER, None),
        ),
        out_specs=(
            P(),
            P(LAYER, None, FEAT),
            P(LAYER, FEAT),
            P(LAYER, None, FEAT, None),
            P(LAYER, None),
        ),
        check_vma=False,
    )
```

```python
import jax
import jax.numpy as jnp
from jax import lax
from jax.experimental import pallas as pl
from jax.experimental.pallas import tpu as pltpu
from jax.sharding import Mesh
from jax.sharding import PartitionSpec as P

MESH = pl.DeviceIdType.MESH
BF16, F32 = jnp.bfloat16, jnp.float32
LAYER = ("x", "yh")
FEAT = ("yl", "z", "c")
NX, NZ = 4, 8

BLOCKS = (
    ((0, 0), (1, 0), (0, 1), (0, -1)),
    ((0, 2), (0, -2), (1, 1), (1, -1)),
    ((1, 2), (1, -2), (1, 3), (1, -3)),
    ((0, 4), (0, 3), (0, -3), (1, 4)),
)
SLOTS = tuple(slot for block in BLOCKS for slot in block)
PLACE = {slot: (b, k) for b, block in enumerate(BLOCKS) for k, slot in enumerate(block)}
OWN = (0, 0)


def own_tree(half, far):
    edges = {
        (0, 2): (OWN, "++"), (0, -2): (OWN, "--"), (1, 0): (OWN, "y"),
        (0, 1): (OWN, "+"), (0, -1): (OWN, "-"),
        (0, 3): ((0, 2), "+"), (0, -3): ((0, -2), "-"),
        (0, 4): ((0, 2), "++") if far == "+" else ((0, -2), "--"),
        (1, 1): ((1, 0), "+"), (1, -1): ((1, 0), "-"),
        (1, 2): ((0, 2), "y"), (1, -2): ((0, -2), "y"),
        (1, 3): ((0, 3), "y"), (1, -3): ((0, -3), "y"), (1, 4): ((0, 4), "y"),
    }
    return {(half, s): ((half, p), way) for s, (p, way) in edges.items()}


def next_tree():
    crossing = ((1, 2), (1, -2), (0, 0), (1, 0), (1, 1), (1, -1), (0, 2), (0, -2))
    edges = {
        (1, 3): ((1, 2), "+"), (1, -3): ((1, -2), "-"), (1, 4): ((1, -2), "--"),
        (0, 1): ((0, 0), "+"), (0, -1): ((0, 0), "-"),
        (0, 3): ((1, 3), "y"), (0, -3): ((1, -3), "y"), (0, 4): ((1, 4), "y"),
    }
    return {(1, (dy, dz)): ((0, (1 - dy, dz)), "cross") for dy, dz in crossing} | {
        (1, s): ((1, p), way) for s, (p, way) in edges.items()
    }


INPUT_TREE = own_tree(0, "+") | own_tree(1, "-")
ERROR_TREE = next_tree() | own_tree(0, "+")
OWN_WAVES = (
    (OWN,),
    ((0, 2), (0, -2), (1, 0), (0, 1), (0, -1)),
    ((0, 3), (0, -3), (0, 4), (1, 1), (1, -1), (1, 2), (1, -2)),
    ((1, 3), (1, -3), (1, 4)),
)
NEXT_WAVES = (
    ((1, 0),),
    ((1, 2), (1, -2), (0, 0), (1, 1), (1, -1)),
    ((1, 3), (1, -3), (1, 4), (0, 1), (0, -1), (0, 2), (0, -2)),
    ((0, 3), (0, -3), (0, 4)),
)


def children_of(tree, node):
    return tuple(child for child, (parent, _) in tree.items() if parent == node)


def main_kernel(
    x_hbm, t_hbm, ew_hbm, eb_hbm, dw_hbm, db_hbm,
    tok, acts, gr1, dpre, dg0, sums, loss_sum,
    ew, dw, eb, db, tg, pre, part, sib_out, sib_in, arr, snd, zeros, gr0, back, dg_sum,
    squares, loss_all,
    load_sem, tok_s, tok_r, tsib_s, tsib_r, psib_s, psib_r, red_s, red_r,
    gr_s, gr_r, gsib_s, gsib_r, loss_s, loss_r,
):
    x, yh = lax.axis_index("x"), lax.axis_index("yh")
    yl, z, c = lax.axis_index("yl"), lax.axis_index("z"), lax.axis_index("c")
    layer = x * 2 + yh
    width = dw.shape[2]
    half_width = width // 2

    to = {
        "+": {"z": lax.rem(z + 1, NZ)},
        "++": {"z": lax.rem(z + 2, NZ)},
        "-": {"z": lax.rem(z + NZ - 1, NZ)},
        "--": {"z": lax.rem(z + NZ - 2, NZ)},
        "y": {"yl": 1 - yl},
        "cross": {"x": lax.rem(x + yh + NX - 1, NX), "yh": 1 - yh, "yl": 1 - yl},
    }
    back_to = {
        "+": to["-"], "++": to["--"], "-": to["+"], "--": to["++"], "y": to["y"],
        "cross": {"x": lax.rem(x + yh, NX), "yh": 1 - yh, "yl": 1 - yl},
    }
    sibling = {"c": 1 - c}
    peers = [
        {"x": lax.rem(x + k // 2, NX), "yh": lax.rem(yh + k % 2, 2)} for k in range(1, 2 * NX)
    ]

    def load(k, src, dst):
        copy = pltpu.make_async_copy(src, dst, load_sem.at[k])
        copy.start()
        return copy

    zeros[...] = jnp.zeros_like(zeros)
    own_loads = [
        load(h, x_hbm.at[0, :, pl.ds(h * half_width, half_width)], tok.at[h, 0, 0, 0])
        for h in (0, 1)
    ]
    ew_load = load(2, ew_hbm.at[0], ew)
    eb_load = load(3, eb_hbm, eb)
    dw_loads = [load(4 + r, dw_hbm.at[0, r], dw.at[r]) for r in (1, 0)]
    tg_load = load(6, t_hbm.at[0], tg)
    db_load = load(7, db_hbm, db)

    barrier = pltpu.get_barrier_semaphore()
    greeted = [*to.values(), back_to["cross"], sibling, *peers]
    for device in greeted:
        pl.semaphore_signal(barrier, inc=1, device_id=device, device_id_type=MESH)
    pl.semaphore_wait(barrier, len(greeted))

    def remote(src, dst, send_sem, recv_sem, device):
        return pltpu.make_async_remote_copy(
            src_ref=src, dst_ref=dst, send_sem=send_sem, recv_sem=recv_sem,
            device_id=device, device_id_type=MESH,
        )

    sent = []

    def gather(tree, buf, ici_s, ici_r, sib_s, sib_r):
        ici, sib = {}, {}
        for h in (0, 1):
            for s in SLOTS:
                b, k = PLACE[s]
                sib[h, s] = remote(
                    buf[h].at[b, 0, k], buf[h].at[b, 1, k],
                    sib_s.at[h, b, k], sib_r.at[h, b, k], sibling,
                )

        def hop(node):
            (ph, parent), way = tree[node]
            h, s = node
            b, k = PLACE[s]
            pb, pk = PLACE[parent]
            sems = ici_s.at[h, b, k], ici_r.at[h, b, k]
            ici[node] = remote(buf[ph].at[pb, 0, pk], buf[h].at[b, 0, k], *sems, to[way])
            if way == "cross":
                blank = remote(zeros, buf[h].at[b, 0, k], *sems, to[way])
                pl.when(layer == 0)(blank.start)
                pl.when(layer != 0)(ici[node].start)
            else:
                ici[node].start()
            sent.append(ici[node])

        def stage(h, slots):
            for s in slots:
                if (h, s) in tree:
                    ici[h, s].wait_recv()
                for child in children_of(tree, (h, s)):
                    hop(child)
                sib[h, s].start()
                sent.append(sib[h, s])

        def settle(h, b):
            for s in BLOCKS[b]:
                sib[h, s].wait_recv()

        return stage, settle

    stage, settle = gather(INPUT_TREE, (tok.at[0], tok.at[1]), tok_s, tok_r, tsib_s, tsib_r)

    def encode(first, blocks):
        rows = pl.ds(first * 128, blocks * 128)
        for h in (0, 1):
            for b in range(first, first + blocks):
                settle(h, b)
        value = eb[...] + jnp.zeros((blocks * 128, 1), F32)
        for h in (0, 1):
            value += jnp.dot(
                tok[h, first : first + blocks].reshape(blocks * 128, half_width),
                ew[h * half_width : (h + 1) * half_width],
                preferred_element_type=F32,
            )
        value = jnp.maximum(value, 0.0)
        pre[rows] = value
        acts[rows] = (value * value).astype(BF16)

    psib = {
        (h, p): remote(
            sib_out.at[h, pl.ds(2 * p, 2)], sib_in.at[h, pl.ds(2 * p, 2)],
            psib_s.at[h, p], psib_r.at[h, p], sibling,
        )
        for h in (0, 1)
        for p in (0, 1)
    }
    tile = 512

    def decode(p):
        for h in (1, 0):

            @pl.loop(0, width // tile)
            def _(j):
                columns = pl.ds(pl.multiple_of(j * tile, tile), tile)
                value = jnp.dot(
                    acts[pl.ds(p * 256, 256)], dw[h, :, columns], preferred_element_type=F32
                ).reshape(2, 2, 4, 16, tile)
                for b in (0, 1):
                    part[h, 2 * p + b, :, :, columns] = value[b, 0]
                    sib_out[h, 2 * p + b, :, :, columns] = value[b, 1].astype(BF16)

            psib[h, p].start()
            sent.append(psib[h, p])

    red = {}
    for (h, s), (_, way) in ERROR_TREE.items():
        b, k = PLACE[s]
        red[h, s] = remote(
            snd.at[h, b, k], arr.at[h, b, k], red_s.at[h, b, k], red_r.at[h, b, k], back_to[way]
        )

    def total(h, s):
        b, k = PLACE[s]
        value = part[h, b, k] + sib_in[h, b, k].astype(F32)
        for child in children_of(ERROR_TREE, (h, s)):
            red[child].wait_recv()
            cb, ck = PLACE[child[1]]
            term = arr[child[0], cb, ck].astype(F32)
            if ERROR_TREE[child][1] == "cross":
                term = jnp.where(layer == 0, 0.0, term)
            value += term
        return value

    def pass_on(h, *slots):
        for s in slots:
            b, k = PLACE[s]
            snd[h, b, k] = total(h, s).astype(BF16)
            red[h, s].start()
            sent.append(red[h, s])

    for h in (0, 1):
        own_loads[h].wait()
        stage(h, OWN_WAVES[0])
    for h in (0, 1):
        stage(h, OWN_WAVES[1])
    ew_load.wait()
    eb_load.wait()
    for h in (0, 1):
        stage(h, OWN_WAVES[2])
    encode(0, 2)
    for load_ in dw_loads:
        load_.wait()
    decode(0)
    for h in (0, 1):
        stage(h, OWN_WAVES[3])
    psib[1, 0].wait_recv()
    pass_on(1, (0, 2), (0, -2), (0, 1), (0, -1), (1, 1), (1, -1), (1, 0))
    psib[0, 0].wait_recv()
    pass_on(0, (1, 1), (1, -1))
    encode(2, 2)
    decode(1)
    pass_on(1, (0, 0))
    psib[1, 1].wait_recv()
    pass_on(1, (0, 3), (0, -3), (0, 4))
    psib[0, 1].wait_recv()
    pass_on(0, (1, 3), (1, -3), (1, 4), (1, 2), (1, -2))
    pass_on(1, (1, 3), (1, -3), (1, 4))
    pass_on(0, (0, 3), (0, -3), (0, 4))
    pass_on(0, (0, 1), (0, -1), (1, 0))
    pass_on(1, (1, 2), (1, -2))
    tg_load.wait()
    db_load.wait()
    pass_on(0, (0, 2), (0, -2))
    gr0[0, 0, 0] = (total(0, OWN) + db[...] - tg[...].astype(F32)).astype(BF16)

    stage, settle = gather(ERROR_TREE, (gr0, gr1), gr_s, gr_r, gsib_s, gsib_r)
    gr = (gr0, gr1)

    def through(h, first, blocks):
        rows = pl.ds(first * 128, blocks * 128)
        for b in range(first, first + blocks):
            settle(h, b)
        value = lax.dot_general(
            gr[h][first : first + blocks].reshape(blocks * 128, width), dw[h],
            (((1,), (1,)), ((), ())), preferred_element_type=F32,
        )
        if h == 0:
            back[rows] = value
        else:
            dpre[rows] = ((value + back[rows]) * 2.0 * pre[rows]).astype(BF16)

    def decoder_grad(p):
        @pl.loop(0, width // tile)
        def _(j):
            columns = pl.ds(pl.multiple_of(j * tile, tile), tile)
            value = lax.dot_general(
                acts[pl.ds(p * 256, 256)],
                gr0[2 * p : 2 * p + 2, :, :, :, columns].reshape(256, tile),
                (((0,), (0,)), ((), ())), preferred_element_type=F32,
            )
            if p == 0:
                dg_sum[:, columns] = value
            else:
                dg0[:, columns] = (value + dg_sum[:, columns]).astype(BF16)

    def add_up():
        @pl.loop(0, width // tile)
        def _(j):
            columns = pl.ds(pl.multiple_of(j * tile, tile), tile)
            total_sum = jnp.zeros((8, tile), F32)
            total_sq = jnp.zeros((8, tile), F32)
            for b in range(4):
                for p in range(2):
                    value = gr0[b, p, :, :, columns].astype(F32).reshape(8, 8, tile)
                    total_sum += jnp.sum(value, axis=0)
                    total_sq += jnp.sum(value * value, axis=0)
            sums[:, columns] = total_sum
            squares[:, columns] = total_sq

        value = jnp.zeros((8, 128), F32)
        for j in range(width // 128):
            value += squares[:, j * 128 : (j + 1) * 128]
        loss_all[0] = value

    stage(0, OWN_WAVES[0])
    stage(0, OWN_WAVES[1])
    stage(1, NEXT_WAVES[0])
    stage(0, OWN_WAVES[2])
    stage(1, NEXT_WAVES[1])
    through(0, 0, 2)
    decoder_grad(0)
    stage(0, OWN_WAVES[3])
    stage(1, NEXT_WAVES[2])
    through(0, 2, 2)
    add_up()
    tells = []
    for k, device in enumerate(peers):
        tells.append(
            remote(loss_all.at[0], loss_all.at[k + 1], loss_s.at[k], loss_r.at[k], device)
        )
        tells[-1].start()
    decoder_grad(1)
    stage(1, NEXT_WAVES[3])
    through(1, 0, 3)
    through(1, 3, 1)
    for tell in tells:
        tell.wait_recv()
    sent += tells
    value = loss_all[0]
    for k in range(1, 2 * NX):
        value += loss_all[k]
    loss_sum[...] = value
    for copy in sent:
        copy.wait_send()


def grad_kernel(
    scale, tok, acts, gr1, dpre, dg0, sums, loss, eg_o, ebg_o, dg_o, dbg_o, mean,
    eg, dg, ebg, dbg, sems,
):
    contract = (((0,), (0,)), ((), ()))
    copies = []

    def store(src, dst):
        copies.append(pltpu.make_async_copy(src, dst, sems.at[len(copies)]))
        copies[-1].start()

    store(dg0, dg_o.at[0, 0])
    tokens, half_width = tok.shape[1:]
    tile = 512
    for j in range(2 * half_width // tile):
        at = j * tile
        part = tok[at // half_width, :, at % half_width : at % half_width + tile]
        eg[j] = lax.dot_general(part, dpre[...], contract, preferred_element_type=F32).astype(BF16)
        store(eg.at[j], eg_o.at[0, pl.ds(at, tile)])
    ebg[...] = jnp.sum(dpre[...].astype(F32), axis=0, keepdims=True)
    dbg[...] = jnp.sum(sums[...], axis=0, keepdims=True)
    store(ebg, ebg_o)
    store(dbg, dbg_o)
    for j in range(gr1.shape[1] // tile):
        at = j * tile
        dg[j] = lax.dot_general(
            acts[...], gr1[:, at : at + tile], contract, preferred_element_type=F32
        ).astype(BF16)
        store(dg.at[j], dg_o.at[0, 1, :, pl.ds(at, tile)])
    mean[0, 0] = jnp.sum(loss[...]) * scale
    for copy in copies:
        copy.wait()


def shards(inputs, targets, enc_weight, enc_bias, dec_weight, dec_bias):
    rows, width = inputs.shape[1:]
    feats = enc_weight.shape[2]
    tokens = rows * 32
    half_width = width // 2
    anywhere = pl.BlockSpec(memory_space=pl.ANY)
    here = pl.BlockSpec(memory_space=pltpu.VMEM)
    dma = pltpu.SemaphoreType.DMA
    chunks = (4, 2, 4, rows)
    tok, acts, gr1, dpre, dg0, sums, loss = pl.pallas_call(
        main_kernel,
        out_shape=(
            pltpu.VMEM((2, *chunks, half_width), BF16),
            pltpu.VMEM((tokens, feats), BF16),
            pltpu.VMEM((*chunks, width), BF16),
            pltpu.VMEM((tokens, feats), BF16),
            pltpu.VMEM((feats, width), BF16),
            pltpu.VMEM((8, width), F32),
            pltpu.VMEM((8, 128), F32),
        ),
        in_specs=[anywhere] * 6,
        out_specs=(here,) * 7,
        scratch_shapes=[
            pltpu.VMEM((width, feats), BF16),
            pltpu.VMEM((2, feats, width), BF16),
            pltpu.VMEM((1, feats), F32),
            pltpu.VMEM((1, width), F32),
            pltpu.VMEM((rows, width), BF16),
            pltpu.VMEM((tokens, feats), F32),
            pltpu.VMEM((2, 4, 4, rows, width), F32),
            pltpu.VMEM((2, 4, 4, rows, width), BF16),
            pltpu.VMEM((2, 4, 4, rows, width), BF16),
            pltpu.VMEM((2, 4, 4, rows, width), BF16),
            pltpu.VMEM((2, 4, 4, rows, width), BF16),
            pltpu.VMEM((rows, width), BF16),
            pltpu.VMEM((*chunks, width), BF16),
            pltpu.VMEM((tokens, feats), F32),
            pltpu.VMEM((feats, width), F32),
            pltpu.VMEM((8, width), F32),
            pltpu.VMEM((2 * NX, 8, 128), F32),
            dma((8,)),
            *[dma((2, 4, 4))] * 4,
            *[dma((2, 2))] * 2,
            *[dma((2, 4, 4))] * 2,
            *[dma((2, 4, 4))] * 4,
            *[dma((2 * NX - 1,))] * 2,
        ],
        compiler_params=pltpu.CompilerParams(
            collective_id=0, has_side_effects=True, vmem_limit_bytes=50 * 2**20
        ),
        name="exchange",
    )(inputs, targets, enc_weight, enc_bias, dec_weight, dec_bias)
    tok = tok.reshape(2, tokens, half_width)
    gr1 = gr1.reshape(tokens, width)
    scale = 1.0 / (2 * NX * tokens * width)
    eg, ebg, dg, dbg, mean = pl.pallas_call(
        lambda *refs: grad_kernel(scale, *refs),
        out_shape=(
            jax.ShapeDtypeStruct((1, width, feats), BF16),
            jax.ShapeDtypeStruct((1, feats), F32),
            jax.ShapeDtypeStruct((1, 2, feats, width), BF16),
            jax.ShapeDtypeStruct((1, width), F32),
            jax.ShapeDtypeStruct((1, 1), F32),
        ),
        in_specs=[here] * 7,
        out_specs=(*[anywhere] * 4, pl.BlockSpec(memory_space=pltpu.SMEM)),
        scratch_shapes=[
            pltpu.VMEM((width // 512, 512, feats), BF16),
            pltpu.VMEM((width // 512, feats, 512), BF16),
            pltpu.VMEM((1, feats), F32),
            pltpu.VMEM((1, width), F32),
            dma((3 + 2 * (width // 512),)),
        ],
        compiler_params=pltpu.CompilerParams(vmem_limit_bytes=24 * 2**20),
        name="weight_grads",
    )(tok, acts, gr1, dpre, dg0, sums, loss)
    return mean[0, 0], eg, ebg, dg, dbg


def solution(mesh):
    finer = Mesh(mesh.devices.reshape(NX, 2, 2, NZ, 2), LAYER + FEAT)
    return jax.shard_map(
        shards,
        mesh=finer,
        in_specs=(
            P(LAYER, FEAT, None),
            P(LAYER, FEAT, None),
            P(LAYER, None, FEAT),
            P(LAYER, FEAT),
            P(LAYER, None, FEAT, None),
            P(LAYER, None),
        ),
        out_specs=(
            P(),
            P(LAYER, None, FEAT),
            P(LAYER, FEAT),
            P(LAYER, None, FEAT, None),
            P(LAYER, None),
        ),
        check_vma=False,
    )
```

```python
import jax
import jax.numpy as jnp
from jax import lax
from jax.experimental import pallas as pl
from jax.experimental.pallas import tpu as pltpu
from jax.sharding import Mesh
from jax.sharding import PartitionSpec as P

MESH = pl.DeviceIdType.MESH
BF16, F32 = jnp.bfloat16, jnp.float32
LAYER = ("x", "yh")
FEAT = ("yl", "z", "c")
NX, NZ = 4, 8

BLOCKS = (
    ((0, 0), (1, 0), (0, 1), (0, -1)),
    ((0, 2), (0, -2), (1, 1), (1, -1)),
    ((1, 2), (1, -2), (1, 3), (1, -3)),
    ((0, 4), (0, 3), (0, -3), (1, 4)),
)
SLOTS = tuple(slot for block in BLOCKS for slot in block)
PLACE = {slot: (b, k) for b, block in enumerate(BLOCKS) for k, slot in enumerate(block)}
OWN = (0, 0)


def own_tree(half, far):
    edges = {
        (0, 2): (OWN, "++"), (0, -2): (OWN, "--"), (1, 0): (OWN, "y"),
        (0, 1): (OWN, "+"), (0, -1): (OWN, "-"),
        (0, 3): ((0, 2), "+"), (0, -3): ((0, -2), "-"),
        (0, 4): ((0, 2), "++") if far == "+" else ((0, -2), "--"),
        (1, 1): ((1, 0), "+"), (1, -1): ((1, 0), "-"),
        (1, 2): ((0, 2), "y"), (1, -2): ((0, -2), "y"),
        (1, 3): ((0, 3), "y"), (1, -3): ((0, -3), "y"), (1, 4): ((0, 4), "y"),
    }
    return {(half, s): ((half, p), way) for s, (p, way) in edges.items()}


def next_tree(far):
    crossing = ((1, 2), (1, -2), (0, 0), (1, 0), (1, 1), (1, -1), (0, 2), (0, -2))
    edges = {
        (1, 3): ((1, 2), "+"), (1, -3): ((1, -2), "-"),
        (1, 4): ((1, 2), "++") if far == "+" else ((1, -2), "--"),
        (0, 1): ((0, 0), "+"), (0, -1): ((0, 0), "-"),
        (0, 3): ((1, 3), "y"), (0, -3): ((1, -3), "y"), (0, 4): ((1, 4), "y"),
    }
    return {(1, (dy, dz)): ((0, (1 - dy, dz)), "cross") for dy, dz in crossing} | {
        (1, s): ((1, p), way) for s, (p, way) in edges.items()
    }


INPUT_TREE = own_tree(0, "+") | own_tree(1, "-")
ERROR_TREES = (next_tree("-") | own_tree(0, "+"), next_tree("+") | own_tree(0, "-"))
OWN_WAVES = (
    (OWN,),
    ((0, 2), (0, -2), (1, 0), (0, 1), (0, -1)),
    ((0, 3), (0, -3), (0, 4), (1, 1), (1, -1), (1, 2), (1, -2)),
    ((1, 3), (1, -3), (1, 4)),
)
NEXT_WAVES = (
    ((1, 0),),
    ((1, 2), (1, -2), (0, 0), (1, 1), (1, -1)),
    ((1, 3), (1, -3), (1, 4), (0, 1), (0, -1), (0, 2), (0, -2)),
    ((0, 3), (0, -3), (0, 4)),
)


def children_of(tree, node):
    return tuple(child for child, (parent, _) in tree.items() if parent == node)


def main_kernel(
    x_hbm, t_hbm, ew_hbm, eb_hbm, dw_hbm, db_hbm,
    tok, acts, gr1, dpre, dg0, sums, loss_sum,
    ew, dw, eb, ew2, dw2, eb2, db, tg, pre, acts2, part, arr, snd, zeros, gr0, back, dg_sum,
    squares, loss_all,
    load_sem, tok_s, tok_r, tsib_s, tsib_r, copy_s, copy_r, red_s, red_r,
    gr_s, gr_r, gsib_s, gsib_r, loss_s, loss_r,
):
    x, yh = lax.axis_index("x"), lax.axis_index("yh")
    yl, z, c = lax.axis_index("yl"), lax.axis_index("z"), lax.axis_index("c")
    layer = x * 2 + yh
    width = dw.shape[2]
    half_width = width // 2

    to = {
        "+": {"z": lax.rem(z + 1, NZ)},
        "++": {"z": lax.rem(z + 2, NZ)},
        "-": {"z": lax.rem(z + NZ - 1, NZ)},
        "--": {"z": lax.rem(z + NZ - 2, NZ)},
        "y": {"yl": 1 - yl},
        "cross": {"x": lax.rem(x + yh + NX - 1, NX), "yh": 1 - yh, "yl": 1 - yl},
    }
    back_to = {
        "+": to["-"], "++": to["--"], "-": to["+"], "--": to["++"], "y": to["y"],
        "cross": {"x": lax.rem(x + yh, NX), "yh": 1 - yh, "yl": 1 - yl},
    }
    sibling = {"c": 1 - c}
    peers = [
        {"x": lax.rem(x + k // 2, NX), "yh": lax.rem(yh + k % 2, 2)} for k in range(1, 2 * NX)
    ]

    def load(k, src, dst):
        copy = pltpu.make_async_copy(src, dst, load_sem.at[k])
        copy.start()
        return copy

    zeros[...] = jnp.zeros_like(zeros)
    own_loads = [
        load(h, x_hbm.at[0, :, pl.ds(h * half_width, half_width)], tok.at[h, 0, 0, 0])
        for h in (0, 1)
    ]
    ew_load = load(2, ew_hbm.at[0], ew)
    eb_load = load(3, eb_hbm, eb)
    dw_loads = [load(4 + r, dw_hbm.at[0, r], dw.at[r]) for r in (1, 0)]
    tg_load = load(6, t_hbm.at[0], tg)
    db_load = load(7, db_hbm, db)

    barrier = pltpu.get_barrier_semaphore()
    greeted = [*to.values(), back_to["cross"], sibling, *peers]
    for device in greeted:
        pl.semaphore_signal(barrier, inc=1, device_id=device, device_id_type=MESH)
    pl.semaphore_wait(barrier, len(greeted))

    def remote(src, dst, send_sem, recv_sem, device):
        return pltpu.make_async_remote_copy(
            src_ref=src, dst_ref=dst, send_sem=send_sem, recv_sem=recv_sem,
            device_id=device, device_id_type=MESH,
        )

    sent = []

    def gather(tree, buf, ici_s, ici_r, sib_s, sib_r):
        ici, sib = {}, {}
        for h in (0, 1):
            for s in SLOTS:
                b, k = PLACE[s]
                sib[h, s] = remote(
                    buf[h].at[b, 0, k], buf[h].at[b, 1, k],
                    sib_s.at[h, b, k], sib_r.at[h, b, k], sibling,
                )

        def hop(node):
            (ph, parent), way = tree[node]
            h, s = node
            b, k = PLACE[s]
            pb, pk = PLACE[parent]
            sems = ici_s.at[h, b, k], ici_r.at[h, b, k]
            ici[node] = remote(buf[ph].at[pb, 0, pk], buf[h].at[b, 0, k], *sems, to[way])
            if way == "cross":
                blank = remote(zeros, buf[h].at[b, 0, k], *sems, to[way])
                pl.when(layer == 0)(blank.start)
                pl.when(layer != 0)(ici[node].start)
            else:
                ici[node].start()
            sent.append(ici[node])

        def stage(h, slots):
            for s in slots:
                if (h, s) in tree:
                    ici[h, s].wait_recv()
                late = [n for n in children_of(tree, (h, s)) if not children_of(tree, n)]
                for child in children_of(tree, (h, s)):
                    if child not in late:
                        hop(child)
                for child in late:
                    hop(child)
                sib[h, s].start()
                sent.append(sib[h, s])

        def settle(h, b):
            for s in BLOCKS[b]:
                sib[h, s].wait_recv()

        return stage, settle

    stage, settle = gather(INPUT_TREE, (tok.at[0], tok.at[1]), tok_s, tok_r, tsib_s, tsib_r)

    copies = [
        remote(src, dst, copy_s.at[k], copy_r.at[k], sibling)
        for k, (src, dst) in enumerate(
            ((ew_hbm.at[0], ew2), (eb_hbm, eb2), (dw_hbm.at[0, 1], dw2.at[1]), (dw_hbm.at[0, 0], dw2.at[0]))
        )
    ]

    def encoded(first, blocks, plane, weight, bias):
        value = bias[...] + jnp.zeros((blocks * 64, 1), F32)
        for h in (0, 1):
            value += jnp.dot(
                tok[h, first : first + blocks, plane].reshape(blocks * 64, half_width),
                weight[h * half_width : (h + 1) * half_width],
                preferred_element_type=F32,
            )
        return jnp.maximum(value, 0.0).reshape(blocks, 64, value.shape[1])

    def encode(first, blocks):
        at = slice(first, first + blocks)
        value = encoded(first, blocks, 0, ew, eb)
        pre[at, 0] = value
        acts[at, 0] = (value * value).astype(BF16)
        value = encoded(first, blocks, 0, ew2, eb2)
        acts2[at] = (value * value).astype(BF16)

    def encode_others():
        for h in (0, 1):
            for b in range(4):
                settle(h, b)
        value = encoded(0, 4, 1, ew, eb)
        pre[:, 1] = value
        acts[:, 1] = (value * value).astype(BF16)

    tile = 512

    def decode(p, q):
        for h in (1, 0):

            @pl.loop(0, half_width // tile)
            def _(j):
                columns = pl.ds(pl.multiple_of(j * tile, tile), tile)
                whole = pl.ds(pl.multiple_of(q * half_width + j * tile, tile), tile)
                value = jnp.dot(
                    acts[2 * p : 2 * p + 2, 0].reshape(128, acts.shape[3]),
                    dw[h, :, whole],
                    preferred_element_type=F32,
                )
                value += jnp.dot(
                    acts2[2 * p : 2 * p + 2].reshape(128, acts.shape[3]),
                    dw2[h, :, whole],
                    preferred_element_type=F32,
                )
                part[q, h, 2 * p : 2 * p + 2, :, :, columns] = value.reshape(2, 4, 16, tile)

    red = {}
    for q in (0, 1):
        for (h, s), (_, way) in ERROR_TREES[q].items():
            b, k = PLACE[s]
            red[q, h, s] = remote(
                snd.at[q, h, b, k], arr.at[q, h, b, k],
                red_s.at[q, h, b, k], red_r.at[q, h, b, k], back_to[way],
            )

    def total(q, h, s):
        b, k = PLACE[s]
        value = part[q, h, b, k]
        for child in children_of(ERROR_TREES[q], (h, s)):
            ch, cs = child
            red[q, ch, cs].wait_recv()
            cb, ck = PLACE[cs]
            term = arr[q, ch, cb, ck].astype(F32)
            if ERROR_TREES[q][child][1] == "cross":
                term = jnp.where(layer == 0, 0.0, term)
            value += term
        return value

    def pass_on(q, h, *slots):
        for s in slots:
            b, k = PLACE[s]
            snd[q, h, b, k] = total(q, h, s).astype(BF16)
            red[q, h, s].start()
            sent.append(red[q, h, s])

    for h in (0, 1):
        own_loads[h].wait()
        stage(h, OWN_WAVES[0])
    for copy in copies:
        copy.start()
    sent += copies
    for h in (0, 1):
        stage(h, ((0, 2), (0, -2), (1, 0)))
    for h in (0, 1):
        stage(h, ((0, 1), (0, -1)))
    ew_load.wait()
    eb_load.wait()
    for h in (0, 1):
        stage(h, ((0, 3), (0, -3), (0, 4)))
    for h in (0, 1):
        stage(h, ((1, 1), (1, -1), (1, 2), (1, -2)))
    copies[0].wait_recv()
    copies[1].wait_recv()
    encode(0, 2)
    for load_ in dw_loads:
        load_.wait()
    copies[2].wait_recv()
    copies[3].wait_recv()
    for q in (0, 1):
        decode(0, q)
    for h in (0, 1):
        stage(h, OWN_WAVES[3])
    for q in (0, 1):
        pass_on(q, 1, (0, 2), (0, -2), (0, 1), (0, -1), (1, 1), (1, -1), (1, 0))
    encode(2, 2)
    for q in (0, 1):
        decode(1, q)
    for q in (0, 1):
        pass_on(q, 1, (0, 3), (0, -3), (0, 4))
    for q in (0, 1):
        pass_on(q, 0, (1, 3), (1, -3), (1, 4))
    for q in (0, 1):
        pass_on(q, 1, (0, 0))
        pass_on(q, 0, (1, 1), (1, -1))
    encode_others()
    for q in (0, 1):
        pass_on(q, 1, (1, 3), (1, -3), (1, 4))
    for q in (0, 1):
        pass_on(q, 0, (1, 2), (1, -2))
    for q in (0, 1):
        pass_on(q, 0, (0, 3), (0, -3), (0, 4))
    for q in (0, 1):
        pass_on(q, 1, (1, 2), (1, -2))
    for q in (0, 1):
        pass_on(q, 0, (0, 1), (0, -1), (1, 0))
    tg_load.wait()
    db_load.wait()
    for q in (0, 1):
        pass_on(q, 0, (0, 2), (0, -2))

    gr = (gr0, gr1)
    stages, settles = [], []
    for q in (0, 1):
        stage, settle = gather(
            ERROR_TREES[q], (gr0.at[q], gr1.at[q]),
            gr_s.at[q], gr_r.at[q], gsib_s.at[q], gsib_r.at[q],
        )
        stages.append(stage)
        settles.append(settle)

    def through(h, first, blocks):
        rows = pl.ds(first * 128, blocks * 128)
        value = back[rows] if h == 1 else 0.0
        for q in (0, 1):
            for b in range(first, first + blocks):
                settles[q](h, b)
            value += lax.dot_general(
                gr[h][q, first : first + blocks].reshape(blocks * 128, half_width),
                dw[h, :, q * half_width : (q + 1) * half_width],
                (((1,), (1,)), ((), ())), preferred_element_type=F32,
            )
        if h == 0:
            back[rows] = value
        else:
            rectified = pre[first : first + blocks].reshape(value.shape)
            dpre[rows] = (value * 2.0 * rectified).astype(BF16)

    def decoder_grad(p):
        for q in (0, 1):

            @pl.loop(0, half_width // tile)
            def _(j):
                columns = pl.ds(pl.multiple_of(j * tile, tile), tile)
                whole = pl.ds(pl.multiple_of(q * half_width + j * tile, tile), tile)
                value = lax.dot_general(
                    acts[2 * p : 2 * p + 2].reshape(256, acts.shape[3]),
                    gr0[q, 2 * p : 2 * p + 2, :, :, :, columns].reshape(256, tile),
                    (((0,), (0,)), ((), ())), preferred_element_type=F32,
                )
                if p == 0:
                    dg_sum[:, whole] = value
                else:
                    dg0[:, whole] = (value + dg_sum[:, whole]).astype(BF16)

    def add_up():
        for q in (0, 1):

            @pl.loop(0, half_width // tile)
            def _(j):
                columns = pl.ds(pl.multiple_of(j * tile, tile), tile)
                whole = pl.ds(pl.multiple_of(q * half_width + j * tile, tile), tile)
                total_sum = jnp.zeros((8, tile), F32)
                total_sq = jnp.zeros((8, tile), F32)
                for b in range(4):
                    for p in range(2):
                        value = gr0[q, b, p, :, :, columns].astype(F32).reshape(8, 8, tile)
                        total_sum += jnp.sum(value, axis=0)
                        total_sq += jnp.sum(value * value, axis=0)
                sums[:, whole] = total_sum
                squares[:, whole] = total_sq

        value = jnp.zeros((8, 128), F32)
        for j in range(width // 128):
            value += squares[:, j * 128 : (j + 1) * 128]
        loss_all[0] = value

    for q in (0, 1):
        columns = slice(q * half_width, (q + 1) * half_width)
        error = total(q, 0, OWN) + db[:, columns] - tg[:, columns].astype(F32)
        gr0[q, 0, 0, 0] = error.astype(BF16)
        stages[q](0, OWN_WAVES[0])
    for q in (0, 1):
        stages[q](0, ((0, 2), (0, -2), (1, 0)))
    for q in (0, 1):
        stages[q](0, ((0, 1), (0, -1)))
        stages[q](1, NEXT_WAVES[0])
    for q in (0, 1):
        stages[q](1, ((1, 2), (1, -2), (0, 0)))
        stages[q](0, ((0, 3), (0, -3), (0, 4)))
    for q in (0, 1):
        stages[q](0, ((1, 1), (1, -1), (1, 2), (1, -2)))
        stages[q](1, ((1, 1), (1, -1)))
    through(0, 0, 2)
    decoder_grad(0)
    for q in (0, 1):
        stages[q](1, ((1, 3), (1, -3), (1, 4)))
    for q in (0, 1):
        stages[q](0, OWN_WAVES[3])
        stages[q](1, ((0, 1), (0, -1), (0, 2), (0, -2)))
    through(0, 2, 2)
    add_up()
    tells = []
    for k, device in enumerate(peers):
        tells.append(
            remote(loss_all.at[0], loss_all.at[k + 1], loss_s.at[k], loss_r.at[k], device)
        )
        tells[-1].start()
    decoder_grad(1)
    for q in (0, 1):
        stages[q](1, NEXT_WAVES[3])
    through(1, 0, 3)
    through(1, 3, 1)
    for tell in tells:
        tell.wait_recv()
    sent += tells
    value = loss_all[0]
    for k in range(1, 2 * NX):
        value += loss_all[k]
    loss_sum[...] = value
    for copy in sent:
        copy.wait_send()


def grad_kernel(
    scale, tok, acts, gr1, dpre, dg0, sums, loss, eg_o, ebg_o, dg_o, dbg_o, mean,
    eg, dg, ebg, dbg, sems,
):
    contract = (((0,), (0,)), ((), ()))
    copies = []

    def store(src, dst):
        copies.append(pltpu.make_async_copy(src, dst, sems.at[len(copies)]))
        copies[-1].start()

    store(dg0, dg_o.at[0, 0])
    tokens, half_width = tok.shape[1:]
    tile = 512
    for j in range(2 * half_width // tile):
        at = j * tile
        part = tok[at // half_width, :, at % half_width : at % half_width + tile]
        eg[j] = lax.dot_general(part, dpre[...], contract, preferred_element_type=F32).astype(BF16)
        store(eg.at[j], eg_o.at[0, pl.ds(at, tile)])
    ebg[...] = jnp.sum(dpre[...].astype(F32), axis=0, keepdims=True)
    dbg[...] = jnp.sum(sums[...], axis=0, keepdims=True)
    store(ebg, ebg_o)
    store(dbg, dbg_o)
    for j in range(2 * half_width // tile):
        at = j * tile
        part = gr1[at // half_width, :, at % half_width : at % half_width + tile]
        dg[j] = lax.dot_general(acts[...], part, contract, preferred_element_type=F32).astype(BF16)
        store(dg.at[j], dg_o.at[0, 1, :, pl.ds(at, tile)])
    mean[0, 0] = jnp.sum(loss[...]) * scale
    for copy in copies:
        copy.wait()


def shards(inputs, targets, enc_weight, enc_bias, dec_weight, dec_bias):
    rows, width = inputs.shape[1:]
    feats = enc_weight.shape[2]
    tokens = rows * 32
    half_width = width // 2
    anywhere = pl.BlockSpec(memory_space=pl.ANY)
    here = pl.BlockSpec(memory_space=pltpu.VMEM)
    dma = pltpu.SemaphoreType.DMA
    chunks = (4, 2, 4, rows)
    tok, acts, gr1, dpre, dg0, sums, loss = pl.pallas_call(
        main_kernel,
        out_shape=(
            pltpu.VMEM((2, *chunks, half_width), BF16),
            pltpu.VMEM((4, 2, tokens // 8, feats), BF16),
            pltpu.VMEM((2, *chunks, half_width), BF16),
            pltpu.VMEM((tokens, feats), BF16),
            pltpu.VMEM((feats, width), BF16),
            pltpu.VMEM((8, width), F32),
            pltpu.VMEM((8, 128), F32),
        ),
        in_specs=[anywhere] * 6,
        out_specs=(here,) * 7,
        scratch_shapes=[
            pltpu.VMEM((width, feats), BF16),
            pltpu.VMEM((2, feats, width), BF16),
            pltpu.VMEM((1, feats), F32),
            pltpu.VMEM((width, feats), BF16),
            pltpu.VMEM((2, feats, width), BF16),
            pltpu.VMEM((1, feats), F32),
            pltpu.VMEM((1, width), F32),
            pltpu.VMEM((rows, width), BF16),
            pltpu.VMEM((4, 2, tokens // 8, feats), F32),
            pltpu.VMEM((4, tokens // 8, feats), BF16),
            pltpu.VMEM((2, 2, 4, 4, rows, half_width), F32),
            pltpu.VMEM((2, 2, 4, 4, rows, half_width), BF16),
            pltpu.VMEM((2, 2, 4, 4, rows, half_width), BF16),
            pltpu.VMEM((rows, half_width), BF16),
            pltpu.VMEM((2, *chunks, half_width), BF16),
            pltpu.VMEM((tokens, feats), F32),
            pltpu.VMEM((feats, width), F32),
            pltpu.VMEM((8, width), F32),
            pltpu.VMEM((2 * NX, 8, 128), F32),
            dma((8,)),
            *[dma((2, 4, 4))] * 4,
            *[dma((4,))] * 2,
            *[dma((2, 2, 4, 4))] * 6,
            *[dma((2 * NX - 1,))] * 2,
        ],
        compiler_params=pltpu.CompilerParams(
            collective_id=0, has_side_effects=True, vmem_limit_bytes=50 * 2**20
        ),
        name="exchange",
    )(inputs, targets, enc_weight, enc_bias, dec_weight, dec_bias)
    tok = tok.reshape(2, tokens, half_width)
    acts = acts.reshape(tokens, feats)
    gr1 = gr1.reshape(2, tokens, half_width)
    scale = 1.0 / (2 * NX * tokens * width)
    eg, ebg, dg, dbg, mean = pl.pallas_call(
        lambda *refs: grad_kernel(scale, *refs),
        out_shape=(
            jax.ShapeDtypeStruct((1, width, feats), BF16),
            jax.ShapeDtypeStruct((1, feats), F32),
            jax.ShapeDtypeStruct((1, 2, feats, width), BF16),
            jax.ShapeDtypeStruct((1, width), F32),
            jax.ShapeDtypeStruct((1, 1), F32),
        ),
        in_specs=[here] * 7,
        out_specs=(*[anywhere] * 4, pl.BlockSpec(memory_space=pltpu.SMEM)),
        scratch_shapes=[
            pltpu.VMEM((width // 512, 512, feats), BF16),
            pltpu.VMEM((width // 512, feats, 512), BF16),
            pltpu.VMEM((1, feats), F32),
            pltpu.VMEM((1, width), F32),
            dma((3 + 2 * (width // 512),)),
        ],
        compiler_params=pltpu.CompilerParams(vmem_limit_bytes=24 * 2**20),
        name="weight_grads",
    )(tok, acts, gr1, dpre, dg0, sums, loss)
    return mean[0, 0], eg, ebg, dg, dbg


def solution(mesh):
    finer = Mesh(mesh.devices.reshape(NX, 2, 2, NZ, 2), LAYER + FEAT)
    return jax.shard_map(
        shards,
        mesh=finer,
        in_specs=(
            P(LAYER, FEAT, None),
            P(LAYER, FEAT, None),
            P(LAYER, None, FEAT),
            P(LAYER, FEAT),
            P(LAYER, None, FEAT, None),
            P(LAYER, None),
        ),
        out_specs=(
            P(),
            P(LAYER, None, FEAT),
            P(LAYER, FEAT),
            P(LAYER, None, FEAT, None),
            P(LAYER, None),
        ),
        check_vma=False,
    )
```

```python
import jax
import jax.numpy as jnp
from jax import lax
from jax.experimental import pallas as pl
from jax.experimental.pallas import tpu as pltpu
from jax.sharding import Mesh
from jax.sharding import PartitionSpec as P

MESH = pl.DeviceIdType.MESH
BF16, F32 = jnp.bfloat16, jnp.float32
LAYER = ("x", "yh")
FEAT = ("yl", "z", "c")
NX, NZ = 4, 8

BLOCKS = (
    ((0, 0), (1, 0), (0, 1), (0, -1)),
    ((0, 2), (0, -2), (1, 1), (1, -1)),
    ((1, 2), (1, -2), (1, 3), (1, -3)),
    ((0, 4), (0, 3), (0, -3), (1, 4)),
)
SLOTS = tuple(slot for block in BLOCKS for slot in block)
PLACE = {slot: (b, k) for b, block in enumerate(BLOCKS) for k, slot in enumerate(block)}
OWN = (0, 0)


def own_tree(half, far):
    edges = {
        (0, 2): (OWN, "++"), (0, -2): (OWN, "--"), (1, 0): (OWN, "y"),
        (0, 1): (OWN, "+"), (0, -1): (OWN, "-"),
        (0, 3): ((0, 2), "+"), (0, -3): ((0, -2), "-"),
        (0, 4): ((0, 2), "++") if far == "+" else ((0, -2), "--"),
        (1, 1): ((1, 0), "+"), (1, -1): ((1, 0), "-"),
        (1, 2): ((0, 2), "y"), (1, -2): ((0, -2), "y"),
        (1, 3): ((0, 3), "y"), (1, -3): ((0, -3), "y"), (1, 4): ((0, 4), "y"),
    }
    return {(half, s): ((half, p), way) for s, (p, way) in edges.items()}


def next_tree(far):
    crossing = ((1, 2), (1, -2), (0, 0), (1, 0), (1, 1), (1, -1), (0, 2), (0, -2))
    edges = {
        (1, 3): ((1, 2), "+"), (1, -3): ((1, -2), "-"),
        (1, 4): ((1, 2), "++") if far == "+" else ((1, -2), "--"),
        (0, 1): ((0, 0), "+"), (0, -1): ((0, 0), "-"),
        (0, 3): ((1, 3), "y"), (0, -3): ((1, -3), "y"), (0, 4): ((1, 4), "y"),
    }
    return {(1, (dy, dz)): ((0, (1 - dy, dz)), "cross") for dy, dz in crossing} | {
        (1, s): ((1, p), way) for s, (p, way) in edges.items()
    }


INPUT_TREE = own_tree(0, "+") | own_tree(1, "-")
ERROR_TREES = (next_tree("-") | own_tree(0, "+"), next_tree("+") | own_tree(0, "-"))
OWN_WAVES = (
    (OWN,),
    ((0, 2), (0, -2), (1, 0), (0, 1), (0, -1)),
    ((0, 3), (0, -3), (0, 4), (1, 1), (1, -1), (1, 2), (1, -2)),
    ((1, 3), (1, -3), (1, 4)),
)
NEXT_WAVES = (
    ((1, 0),),
    ((1, 2), (1, -2), (0, 0), (1, 1), (1, -1)),
    ((1, 3), (1, -3), (1, 4), (0, 1), (0, -1), (0, 2), (0, -2)),
    ((0, 3), (0, -3), (0, 4)),
)


def children_of(tree, node):
    return tuple(child for child, (parent, _) in tree.items() if parent == node)


def main_kernel(
    x_hbm, t_hbm, ew_hbm, eb_hbm, dw_hbm, db_hbm,
    tok, acts, gr1, dpre, dg0, sums, loss_sum,
    ew, dw, eb, ew2, dw2, eb2, db, tg, pre, acts2, part, arr, snd, zeros, gr0, back, dg_sum,
    squares, loss_all,
    load_sem, tok_s, tok_r, tsib_s, tsib_r, copy_s, copy_r, red_s, red_r,
    gr_s, gr_r, gsib_s, gsib_r, loss_s, loss_r,
):
    x, yh = lax.axis_index("x"), lax.axis_index("yh")
    yl, z, c = lax.axis_index("yl"), lax.axis_index("z"), lax.axis_index("c")
    layer = x * 2 + yh
    width = dw.shape[2]
    half_width = width // 2

    to = {
        "+": {"z": lax.rem(z + 1, NZ)},
        "++": {"z": lax.rem(z + 2, NZ)},
        "-": {"z": lax.rem(z + NZ - 1, NZ)},
        "--": {"z": lax.rem(z + NZ - 2, NZ)},
        "y": {"yl": 1 - yl},
        "cross": {"x": lax.rem(x + yh + NX - 1, NX), "yh": 1 - yh, "yl": 1 - yl},
    }
    back_to = {
        "+": to["-"], "++": to["--"], "-": to["+"], "--": to["++"], "y": to["y"],
        "cross": {"x": lax.rem(x + yh, NX), "yh": 1 - yh, "yl": 1 - yl},
    }
    sibling = {"c": 1 - c}
    peers = [
        {"x": lax.rem(x + k // 2, NX), "yh": lax.rem(yh + k % 2, 2)} for k in range(1, 2 * NX)
    ]

    def load(k, src, dst):
        copy = pltpu.make_async_copy(src, dst, load_sem.at[k])
        copy.start()
        return copy

    zeros[...] = jnp.zeros_like(zeros)
    own_loads = [
        load(h, x_hbm.at[0, :, pl.ds(h * half_width, half_width)], tok.at[h, 0, 0, 0])
        for h in (0, 1)
    ]
    ew_load = load(2, ew_hbm.at[0], ew)
    eb_load = load(3, eb_hbm, eb)
    dw_loads = [load(4 + r, dw_hbm.at[0, r], dw.at[r]) for r in (1, 0)]
    tg_load = load(6, t_hbm.at[0], tg)
    db_load = load(7, db_hbm, db)

    barrier = pltpu.get_barrier_semaphore()
    greeted = [*to.values(), back_to["cross"], sibling, *peers]
    for device in greeted:
        pl.semaphore_signal(barrier, inc=1, device_id=device, device_id_type=MESH)
    pl.semaphore_wait(barrier, len(greeted))

    def remote(src, dst, send_sem, recv_sem, device):
        return pltpu.make_async_remote_copy(
            src_ref=src, dst_ref=dst, send_sem=send_sem, recv_sem=recv_sem,
            device_id=device, device_id_type=MESH,
        )

    sent = []

    def gather(tree, buf, ici_s, ici_r, sib_s, sib_r):
        ici, sib = {}, {}
        for h in (0, 1):
            for s in SLOTS:
                b, k = PLACE[s]
                sib[h, s] = remote(
                    buf[h].at[b, 0, k], buf[h].at[b, 1, k],
                    sib_s.at[h, b, k], sib_r.at[h, b, k], sibling,
                )

        def hop(node):
            (ph, parent), way = tree[node]
            h, s = node
            b, k = PLACE[s]
            pb, pk = PLACE[parent]
            sems = ici_s.at[h, b, k], ici_r.at[h, b, k]
            ici[node] = remote(buf[ph].at[pb, 0, pk], buf[h].at[b, 0, k], *sems, to[way])
            if way == "cross":
                blank = remote(zeros, buf[h].at[b, 0, k], *sems, to[way])
                pl.when(layer == 0)(blank.start)
                pl.when(layer != 0)(ici[node].start)
            else:
                ici[node].start()
            sent.append(ici[node])

        def stage(h, slots):
            for s in slots:
                if (h, s) in tree:
                    ici[h, s].wait_recv()
                late = [n for n in children_of(tree, (h, s)) if not children_of(tree, n)]
                for child in children_of(tree, (h, s)):
                    if child not in late:
                        hop(child)
                for child in late:
                    hop(child)
                sib[h, s].start()
                sent.append(sib[h, s])

        def settle(h, b):
            for s in BLOCKS[b]:
                sib[h, s].wait_recv()

        return stage, settle

    stage, settle = gather(INPUT_TREE, (tok.at[0], tok.at[1]), tok_s, tok_r, tsib_s, tsib_r)

    copies = [
        remote(src, dst, copy_s.at[k], copy_r.at[k], sibling)
        for k, (src, dst) in enumerate(
            ((ew_hbm.at[0], ew2), (eb_hbm, eb2), (dw_hbm.at[0, 1], dw2.at[1]), (dw_hbm.at[0, 0], dw2.at[0]))
        )
    ]

    def encoded(first, blocks, plane, weight, bias):
        value = bias[...] + jnp.zeros((blocks * 64, 1), F32)
        for h in (0, 1):
            value += jnp.dot(
                tok[h, first : first + blocks, plane].reshape(blocks * 64, half_width),
                weight[h * half_width : (h + 1) * half_width],
                preferred_element_type=F32,
            )
        return jnp.maximum(value, 0.0).reshape(blocks, 64, value.shape[1])

    def encode(first, blocks):
        at = slice(first, first + blocks)
        value = encoded(first, blocks, 0, ew, eb)
        pre[at, 0] = value
        acts[at, 0] = (value * value).astype(BF16)
        value = encoded(first, blocks, 0, ew2, eb2)
        acts2[at] = (value * value).astype(BF16)

    def encode_others():
        for h in (0, 1):
            for b in range(4):
                settle(h, b)
        value = encoded(0, 4, 1, ew, eb)
        pre[:, 1] = value
        acts[:, 1] = (value * value).astype(BF16)

    tile = 512

    def decode(p, q, halves=(1, 0)):
        for h in halves:

            @pl.loop(0, half_width // tile)
            def _(j):
                columns = pl.ds(pl.multiple_of(j * tile, tile), tile)
                whole = pl.ds(pl.multiple_of(q * half_width + j * tile, tile), tile)
                value = jnp.dot(
                    acts[2 * p : 2 * p + 2, 0].reshape(128, acts.shape[3]),
                    dw[h, :, whole],
                    preferred_element_type=F32,
                )
                value += jnp.dot(
                    acts2[2 * p : 2 * p + 2].reshape(128, acts.shape[3]),
                    dw2[h, :, whole],
                    preferred_element_type=F32,
                )
                part[q, h, 2 * p : 2 * p + 2, :, :, columns] = value.reshape(2, 4, 16, tile)

    red = {}
    for q in (0, 1):
        for (h, s), (_, way) in ERROR_TREES[q].items():
            b, k = PLACE[s]
            red[q, h, s] = remote(
                snd.at[q, h, b, k], arr.at[q, h, b, k],
                red_s.at[q, h, b, k], red_r.at[q, h, b, k], back_to[way],
            )

    def total(q, h, s):
        b, k = PLACE[s]
        value = part[q, h, b, k]
        for child in children_of(ERROR_TREES[q], (h, s)):
            ch, cs = child
            red[q, ch, cs].wait_recv()
            cb, ck = PLACE[cs]
            term = arr[q, ch, cb, ck].astype(F32)
            if ERROR_TREES[q][child][1] == "cross":
                term = jnp.where(layer == 0, 0.0, term)
            value += term
        return value

    def pass_on(q, h, *slots):
        for s in slots:
            b, k = PLACE[s]
            snd[q, h, b, k] = total(q, h, s).astype(BF16)
            red[q, h, s].start()
            sent.append(red[q, h, s])

    for h in (0, 1):
        own_loads[h].wait()
        stage(h, OWN_WAVES[0])
    for copy in copies:
        copy.start()
    sent += copies
    for h in (0, 1):
        stage(h, ((0, 2), (0, -2), (1, 0)))
    for h in (0, 1):
        stage(h, ((0, 1), (0, -1)))
    ew_load.wait()
    eb_load.wait()
    for h in (0, 1):
        stage(h, ((0, 3), (0, -3), (0, 4)))
    for h in (0, 1):
        stage(h, ((1, 1), (1, -1), (1, 2), (1, -2)))
    copies[0].wait_recv()
    copies[1].wait_recv()
    encode(0, 2)
    for load_ in dw_loads:
        load_.wait()
    copies[2].wait_recv()
    copies[3].wait_recv()
    for q in (0, 1):
        decode(0, q, (1,))
        pass_on(q, 1, (0, 2), (0, -2), (0, 1), (0, -1), (1, 1), (1, -1), (1, 0))
    for h in (0, 1):
        stage(h, OWN_WAVES[3])
    encode(2, 2)
    for q in (0, 1):
        decode(1, q, (1,))
        pass_on(q, 1, (0, 3), (0, -3), (0, 4))
    for q in (0, 1):
        decode(1, q, (0,))
    for q in (0, 1):
        pass_on(q, 0, (1, 3), (1, -3), (1, 4))
    for q in (0, 1):
        decode(0, q, (0,))
    for q in (0, 1):
        pass_on(q, 1, (0, 0))
        pass_on(q, 0, (1, 1), (1, -1))
    for q in (0, 1):
        pass_on(q, 1, (1, 3), (1, -3), (1, 4))
    for q in (0, 1):
        pass_on(q, 0, (1, 2), (1, -2))
    for q in (0, 1):
        pass_on(q, 0, (0, 3), (0, -3), (0, 4))
    for q in (0, 1):
        pass_on(q, 1, (1, 2), (1, -2))
    encode_others()
    for q in (0, 1):
        pass_on(q, 0, (0, 1), (0, -1), (1, 0))
    tg_load.wait()
    db_load.wait()
    for q in (0, 1):
        pass_on(q, 0, (0, 2), (0, -2))

    gr = (gr0, gr1)
    stages, settles = [], []
    for q in (0, 1):
        stage, settle = gather(
            ERROR_TREES[q], (gr0.at[q], gr1.at[q]),
            gr_s.at[q], gr_r.at[q], gsib_s.at[q], gsib_r.at[q],
        )
        stages.append(stage)
        settles.append(settle)

    def through(h, first, blocks):
        rows = pl.ds(first * 128, blocks * 128)
        value = back[rows] if h == 1 else 0.0
        for q in (0, 1):
            for b in range(first, first + blocks):
                settles[q](h, b)
            value += lax.dot_general(
                gr[h][q, first : first + blocks].reshape(blocks * 128, half_width),
                dw[h, :, q * half_width : (q + 1) * half_width],
                (((1,), (1,)), ((), ())), preferred_element_type=F32,
            )
        if h == 0:
            back[rows] = value
        else:
            rectified = pre[first : first + blocks].reshape(value.shape)
            dpre[rows] = (value * 2.0 * rectified).astype(BF16)

    def decoder_grad(p):
        for q in (0, 1):

            @pl.loop(0, half_width // tile)
            def _(j):
                columns = pl.ds(pl.multiple_of(j * tile, tile), tile)
                whole = pl.ds(pl.multiple_of(q * half_width + j * tile, tile), tile)
                value = lax.dot_general(
                    acts[2 * p : 2 * p + 2].reshape(256, acts.shape[3]),
                    gr0[q, 2 * p : 2 * p + 2, :, :, :, columns].reshape(256, tile),
                    (((0,), (0,)), ((), ())), preferred_element_type=F32,
                )
                if p == 0:
                    dg_sum[:, whole] = value
                else:
                    dg0[:, whole] = (value + dg_sum[:, whole]).astype(BF16)

    def add_up():
        for q in (0, 1):

            @pl.loop(0, half_width // tile)
            def _(j):
                columns = pl.ds(pl.multiple_of(j * tile, tile), tile)
                whole = pl.ds(pl.multiple_of(q * half_width + j * tile, tile), tile)
                total_sum = jnp.zeros((8, tile), F32)
                total_sq = jnp.zeros((8, tile), F32)
                for b in range(4):
                    for p in range(2):
                        value = gr0[q, b, p, :, :, columns].astype(F32).reshape(8, 8, tile)
                        total_sum += jnp.sum(value, axis=0)
                        total_sq += jnp.sum(value * value, axis=0)
                sums[:, whole] = total_sum
                squares[:, whole] = total_sq

        value = jnp.zeros((8, 128), F32)
        for j in range(width // 128):
            value += squares[:, j * 128 : (j + 1) * 128]
        loss_all[0] = value

    for q in (0, 1):
        columns = slice(q * half_width, (q + 1) * half_width)
        error = total(q, 0, OWN) + db[:, columns] - tg[:, columns].astype(F32)
        gr0[q, 0, 0, 0] = error.astype(BF16)
        stages[q](0, OWN_WAVES[0])
    for q in (0, 1):
        stages[q](0, ((0, 2), (0, -2), (1, 0)))
    for q in (0, 1):
        stages[q](0, ((0, 1), (0, -1)))
        stages[q](1, NEXT_WAVES[0])
    for q in (0, 1):
        stages[q](1, ((1, 2), (1, -2), (0, 0)))
        stages[q](0, ((0, 3), (0, -3), (0, 4)))
    for q in (0, 1):
        stages[q](0, ((1, 1), (1, -1), (1, 2), (1, -2)))
        stages[q](1, ((1, 1), (1, -1)))
    through(0, 0, 2)
    decoder_grad(0)
    for q in (0, 1):
        stages[q](1, ((1, 3), (1, -3), (1, 4)))
    for q in (0, 1):
        stages[q](0, OWN_WAVES[3])
        stages[q](1, ((0, 1), (0, -1), (0, 2), (0, -2)))
    through(0, 2, 2)
    add_up()
    tells = []
    for k, device in enumerate(peers):
        tells.append(
            remote(loss_all.at[0], loss_all.at[k + 1], loss_s.at[k], loss_r.at[k], device)
        )
        tells[-1].start()
    decoder_grad(1)
    for q in (0, 1):
        stages[q](1, NEXT_WAVES[3])
    through(1, 0, 3)
    through(1, 3, 1)
    for tell in tells:
        tell.wait_recv()
    sent += tells
    value = loss_all[0]
    for k in range(1, 2 * NX):
        value += loss_all[k]
    loss_sum[...] = value
    for copy in sent:
        copy.wait_send()


def grad_kernel(
    scale, tok, acts, gr1, dpre, dg0, sums, loss, eg_o, ebg_o, dg_o, dbg_o, mean,
    eg, dg, ebg, dbg, sems,
):
    contract = (((0,), (0,)), ((), ()))
    copies = []

    def store(src, dst):
        copies.append(pltpu.make_async_copy(src, dst, sems.at[len(copies)]))
        copies[-1].start()

    store(dg0, dg_o.at[0, 0])
    tokens, half_width = tok.shape[1:]
    tile = 512
    for j in range(2 * half_width // tile):
        at = j * tile
        part = tok[at // half_width, :, at % half_width : at % half_width + tile]
        eg[j] = lax.dot_general(part, dpre[...], contract, preferred_element_type=F32).astype(BF16)
        store(eg.at[j], eg_o.at[0, pl.ds(at, tile)])
    ebg[...] = jnp.sum(dpre[...].astype(F32), axis=0, keepdims=True)
    dbg[...] = jnp.sum(sums[...], axis=0, keepdims=True)
    store(ebg, ebg_o)
    store(dbg, dbg_o)
    for j in range(2 * half_width // tile):
        at = j * tile
        part = gr1[at // half_width, :, at % half_width : at % half_width + tile]
        dg[j] = lax.dot_general(acts[...], part, contract, preferred_element_type=F32).astype(BF16)
        store(dg.at[j], dg_o.at[0, 1, :, pl.ds(at, tile)])
    mean[0, 0] = jnp.sum(loss[...]) * scale
    for copy in copies:
        copy.wait()


def shards(inputs, targets, enc_weight, enc_bias, dec_weight, dec_bias):
    rows, width = inputs.shape[1:]
    feats = enc_weight.shape[2]
    tokens = rows * 32
    half_width = width // 2
    anywhere = pl.BlockSpec(memory_space=pl.ANY)
    here = pl.BlockSpec(memory_space=pltpu.VMEM)
    dma = pltpu.SemaphoreType.DMA
    chunks = (4, 2, 4, rows)
    tok, acts, gr1, dpre, dg0, sums, loss = pl.pallas_call(
        main_kernel,
        out_shape=(
            pltpu.VMEM((2, *chunks, half_width), BF16),
            pltpu.VMEM((4, 2, tokens // 8, feats), BF16),
            pltpu.VMEM((2, *chunks, half_width), BF16),
            pltpu.VMEM((tokens, feats), BF16),
            pltpu.VMEM((feats, width), BF16),
            pltpu.VMEM((8, width), F32),
            pltpu.VMEM((8, 128), F32),
        ),
        in_specs=[anywhere] * 6,
        out_specs=(here,) * 7,
        scratch_shapes=[
            pltpu.VMEM((width, feats), BF16),
            pltpu.VMEM((2, feats, width), BF16),
            pltpu.VMEM((1, feats), F32),
            pltpu.VMEM((width, feats), BF16),
            pltpu.VMEM((2, feats, width), BF16),
            pltpu.VMEM((1, feats), F32),
            pltpu.VMEM((1, width), F32),
            pltpu.VMEM((rows, width), BF16),
            pltpu.VMEM((4, 2, tokens // 8, feats), F32),
            pltpu.VMEM((4, tokens // 8, feats), BF16),
            pltpu.VMEM((2, 2, 4, 4, rows, half_width), F32),
            pltpu.VMEM((2, 2, 4, 4, rows, half_width), BF16),
            pltpu.VMEM((2, 2, 4, 4, rows, half_width), BF16),
            pltpu.VMEM((rows, half_width), BF16),
            pltpu.VMEM((2, *chunks, half_width), BF16),
            pltpu.VMEM((tokens, feats), F32),
            pltpu.VMEM((feats, width), F32),
            pltpu.VMEM((8, width), F32),
            pltpu.VMEM((2 * NX, 8, 128), F32),
            dma((8,)),
            *[dma((2, 4, 4))] * 4,
            *[dma((4,))] * 2,
            *[dma((2, 2, 4, 4))] * 6,
            *[dma((2 * NX - 1,))] * 2,
        ],
        compiler_params=pltpu.CompilerParams(
            collective_id=0, has_side_effects=True, vmem_limit_bytes=50 * 2**20
        ),
        name="exchange",
    )(inputs, targets, enc_weight, enc_bias, dec_weight, dec_bias)
    tok = tok.reshape(2, tokens, half_width)
    acts = acts.reshape(tokens, feats)
    gr1 = gr1.reshape(2, tokens, half_width)
    scale = 1.0 / (2 * NX * tokens * width)
    eg, ebg, dg, dbg, mean = pl.pallas_call(
        lambda *refs: grad_kernel(scale, *refs),
        out_shape=(
            jax.ShapeDtypeStruct((1, width, feats), BF16),
            jax.ShapeDtypeStruct((1, feats), F32),
            jax.ShapeDtypeStruct((1, 2, feats, width), BF16),
            jax.ShapeDtypeStruct((1, width), F32),
            jax.ShapeDtypeStruct((1, 1), F32),
        ),
        in_specs=[here] * 7,
        out_specs=(*[anywhere] * 4, pl.BlockSpec(memory_space=pltpu.SMEM)),
        scratch_shapes=[
            pltpu.VMEM((width // 512, 512, feats), BF16),
            pltpu.VMEM((width // 512, feats, 512), BF16),
            pltpu.VMEM((1, feats), F32),
            pltpu.VMEM((1, width), F32),
            dma((3 + 2 * (width // 512),)),
        ],
        compiler_params=pltpu.CompilerParams(vmem_limit_bytes=24 * 2**20),
        name="weight_grads",
    )(tok, acts, gr1, dpre, dg0, sums, loss)
    return mean[0, 0], eg, ebg, dg, dbg


def solution(mesh):
    finer = Mesh(mesh.devices.reshape(NX, 2, 2, NZ, 2), LAYER + FEAT)
    return jax.shard_map(
        shards,
        mesh=finer,
        in_specs=(
            P(LAYER, FEAT, None),
            P(LAYER, FEAT, None),
            P(LAYER, None, FEAT),
            P(LAYER, FEAT),
            P(LAYER, None, FEAT, None),
            P(LAYER, None),
        ),
        out_specs=(
            P(),
            P(LAYER, None, FEAT),
            P(LAYER, FEAT),
            P(LAYER, None, FEAT, None),
            P(LAYER, None),
        ),
        check_vma=False,
    )
```
